256 devices in a mesh: exp: 32 (over y, z_lo, core), feat: 8 (over z_hi, x).
Axes of the slice: x: 4, y: 4, z: 8 (z_hi: 2, z_lo: 4; z = z_hi * 4 + z_lo), core: 2. Of those that a mesh axis runs over, the one named last changes fastest.
Arguments:
- tokens: bfloat16 [512, 7168], P('exp', 'feat'), may hold values from -6 to 6
- route_ids: int32 [512, 8], P('exp'), may hold values from 0 to 31, all different within a row
- route_weights: float32 [512, 8], P('exp'), may hold values from 0.05 to 0.6
- gate_proj: bfloat16 [32, 7168, 1024], P('exp', 'feat'), may hold values from -0.0625 to 0.0625
- up_proj: bfloat16 [32, 7168, 1024], P('exp', 'feat'), may hold values from -0.0625 to 0.0625
- down_proj: bfloat16 [32, 1024, 7168], P('exp', None, 'feat'), may hold values from -0.1875 to 0.1875
- enc_weight: bfloat16 [7168, 65536], P('feat', 'exp'), may hold values from -0.0625 to 0.0625
- enc_bias: float32 [65536], P('exp'), may hold values from -3 to 3
- dec_weight: bfloat16 [65536, 7168], P('exp', 'feat'), may hold values from -0.0234375 to 0.0234375
- dec_bias: float32 [7168], P('feat'), may hold values from -3 to 3
- clamp_ids: int32 [64], replicated, may hold values from 0 to 65535, as said below
- clamp_values: bfloat16 [64], replicated, may hold values from 8 to 30
Outputs:
- error_term: float32 [512, 7168], P('exp', 'feat')
- steered: float32 [512, 7168], P('exp', 'feat')
The draws below stay inside these ranges and needn't reach their ends.
Inputs may be any that keep to these rules, and one draw needn't show every extreme that they name: `route_ids`: each token names 8 different experts. `clamp_ids`: 64 different features.
All inputs are finite; a program needn't handle non-finite values.
Results may differ from the reference program's by a relative error of at most 0.0035.
Values may be sent and summed in bfloat16 or wider, within the bound.
A program may use at most 64 MiB of HBM per device.

```python
import jax
import jax.numpy as jnp
from jax import lax

D = 7168
EFF = 1024
FEATS = 65536
TOP = 8
SLOT = 8
CLAMPS = 64
TOK_DEV = 16
EXPERTS = 32
TOKENS = 512
CAP = 256


def draw_clamp_ids(key, part):
    middle = jax.random.permutation(jax.random.fold_in(key, 1), FEATS - 2)[:CLAMPS - 2].astype(jnp.int32) + 1
    extremes = jnp.array([0, FEATS - 1], dtype=jnp.int32)
    joined = jnp.concatenate([middle, extremes])
    shuffle_order = jax.random.permutation(jax.random.fold_in(key, 2), CLAMPS)
    return joined[shuffle_order].astype(jnp.int32)


def levels(stream_key, extent, pieces, least, high):
    def one(position, parts):
        draws = jax.random.uniform(jax.random.fold_in(jax.random.fold_in(stream_key, 6), position), (parts,), jnp.float32, least / len(pieces), high / len(pieces))
        return jnp.repeat(jnp.exp(draws), extent[position] // parts).reshape((-1,) + (1,) * (len(extent) - position - 1))

    level = one(*pieces[0])
    for cut in pieces[1:]:
        level = level * one(*cut)
    return level


def picks_of(rng, rows, amount, top, lift):
    ranking = jax.random.permutation(jax.random.fold_in(rng, 1), amount)
    boost = ranking
    for power in range(3):
        boost = boost * boost // amount
    boost = boost * lift // amount
    lots = jax.random.randint(jax.random.fold_in(rng, 2), (rows, amount), 0, 4096) + boost
    fixed_rows = jax.random.permutation(jax.random.fold_in(rng, 3), rows)[jnp.arange(amount) % rows]
    lots = jnp.where(jnp.arange(rows)[:, None] == fixed_rows[None, :], 1 << 14, lots)
    score = lots * amount + jnp.arange(amount)
    return lax.top_k(score.astype(jnp.int32), top)[1].astype(jnp.int32)


def gaussian(own_key, extent, scale, limit, shards=(), held_as=jnp.bfloat16):
    values = scale * jax.random.normal(own_key, extent, jnp.float32)
    if shards:
        values = values * levels(own_key, extent, shards, -0.22, 0.18)
    return jnp.clip(values, -limit, limit).astype(held_as)


def setup_inputs(seed: int = 0) -> dict:
    seeds = jax.random.split(jax.random.key(seed), 13)
    return {
        "tokens": gaussian(seeds[0], (TOKENS, D), 1.0, 6.0, ((0, 32), (1, 8))),
        "route_ids": picks_of(seeds[1], TOKENS, EXPERTS, TOP, 4096),
        "route_weights": jnp.clip(0.05 + 0.55 * jax.random.uniform(seeds[2], (TOKENS, TOP), jnp.float32) ** levels(seeds[2], (TOKENS, TOP), ((0, 32),), -0.2, 0.2), 0.05, 0.6),
        "gate_proj": gaussian(seeds[3], (EXPERTS, D, EFF), D ** -0.5, 0.0625, ((0, 32), (1, 8))),
        "up_proj": gaussian(seeds[4], (EXPERTS, D, EFF), D ** -0.5, 0.0625, ((0, 32), (1, 8))),
        "down_proj": gaussian(seeds[5], (EXPERTS, EFF, D), EFF ** -0.5, 0.1875, ((0, 32), (2, 8))),
        "enc_weight": gaussian(seeds[6], (D, FEATS), D ** -0.5, 0.0625, ((0, 8), (1, 32))),
        "enc_bias": gaussian(seeds[7], (FEATS,), 0.5, 3.0, ((0, 32),), jnp.float32),
        "dec_weight": gaussian(seeds[8], (FEATS, D), FEATS ** -0.5, 0.0234375, ((0, 32), (1, 8))),
        "dec_bias": gaussian(seeds[9], (D,), 0.5, 3.0, ((0, 8),), jnp.float32),
        "clamp_ids": draw_clamp_ids(jax.random.fold_in(seeds[12], 71), 0),
        "clamp_values": jnp.clip(jax.random.uniform(seeds[11], (CLAMPS,), jnp.float32, 8.0, 30.0), 8.0, 30.0).astype(jnp.bfloat16),
    }


def route_codes(route_ids):
    total_rows = route_ids.shape[0]
    blocks = total_rows // TOK_DEV
    entries = route_ids.reshape(blocks, TOK_DEV * TOP)
    experts = jnp.arange(EXPERTS, dtype=jnp.int32)
    onehot = (entries[:, :, None] == experts[None, None, :]).astype(jnp.int32)
    before = jnp.sum(jnp.cumsum(onehot, axis=1) * onehot, axis=2) - 1
    retained = before < SLOT
    block_base = (jnp.arange(blocks, dtype=jnp.int32) * SLOT)[:, None]
    slot_code = jnp.where(retained, entries * CAP + block_base + before, EXPERTS * CAP)
    return slot_code.reshape(total_rows, TOP).astype(jnp.int32), retained.reshape(total_rows, TOP)


def one_expert(operands):
    rows_in, gate_w, up_w, down_w = operands
    gate_val = jnp.dot(rows_in, gate_w, preferred_element_type=jnp.float32)
    up_val = jnp.dot(rows_in, up_w, preferred_element_type=jnp.float32)
    hidden = (jax.nn.silu(gate_val) * up_val).astype(jnp.bfloat16)
    return jnp.dot(hidden, down_w, preferred_element_type=jnp.float32).astype(jnp.bfloat16)


def reference(tokens, route_ids, route_weights, gate_proj, up_proj, down_proj, enc_weight, enc_bias, dec_weight, dec_bias, clamp_ids, clamp_values):
    slot_code, retained = route_codes(route_ids)
    flat_code = slot_code.reshape(-1)
    repeated = jnp.repeat(tokens, TOP, axis=0)
    buffers = jnp.zeros((EXPERTS * CAP, D), jnp.bfloat16).at[flat_code].set(repeated, mode="drop")
    buffers = buffers.reshape(EXPERTS, CAP, D)
    expert_out = lax.map(one_expert, (buffers, gate_proj, up_proj, down_proj)).reshape(EXPERTS * CAP, D)
    safe_code = jnp.minimum(flat_code, EXPERTS * CAP - 1).astype(jnp.int32)
    picked = jnp.take(expert_out, safe_code, axis=0).astype(jnp.float32).reshape(TOKENS, TOP, D)
    scales = jnp.where(retained, route_weights, 0.0)
    moe_out = jnp.sum(picked * scales[:, :, None], axis=1)
    pre_act = jnp.dot(tokens, enc_weight, preferred_element_type=jnp.float32) + enc_bias
    feature_act = jax.nn.relu(pre_act).astype(jnp.bfloat16)
    rebuilt = jnp.dot(feature_act, dec_weight, preferred_element_type=jnp.float32)
    chosen = jnp.take(feature_act, clamp_ids, axis=1).astype(jnp.float32)
    change = clamp_values.astype(jnp.float32)[None, :] - chosen
    rows_dec = jnp.take(dec_weight, clamp_ids, axis=0).astype(jnp.float32)
    clamp_shift = jnp.dot(change, rows_dec, precision=lax.Precision.HIGHEST)
    error_term = (moe_out - rebuilt - dec_bias).astype(jnp.float32)
    steered = (moe_out + clamp_shift).astype(jnp.float32)
    return error_term, steered
```

```python
import functools

import jax
import jax.numpy as jnp
from jax import lax
from jax.experimental import pallas as pl
from jax.experimental.pallas import tpu as pltpu
from jax.sharding import PartitionSpec as P

SLOT = 8
ROWS = 16
WIDTH = 896
EXTRA = 128
WIDE = WIDTH + EXTRA
FEATURES = 2048
HIDDEN = 1024
CHIPS = 16
EXPERTS = 32
CHUNKS = 4
CHUNK_ROWS = 128
MESH = pl.DeviceIdType.MESH
F32 = jnp.float32
BF16 = jnp.bfloat16


def remote(src, dst, send_sem, recv_sem, device):
    return pltpu.make_async_remote_copy(
        src_ref=src,
        dst_ref=dst,
        send_sem=send_sem,
        recv_sem=recv_sem,
        device_id=device,
        device_id_type=MESH,
    )


def dot(a, b):
    return jnp.dot(a, b, preferred_element_type=F32)


def kernel(
    tok_ref,
    route_ref,
    weight_ref,
    bias_ref,
    dbias_ref,
    ids_ref,
    values_ref,
    gate_hbm,
    up_hbm,
    down_hbm,
    enc_hbm,
    dec_hbm,
    err_ref,
    steered_ref,
    gate_w,
    up_w,
    down_w,
    enc_w,
    dec_w,
    tok_all,
    gu_own,
    gu_in,
    gu_zsend,
    gu_zin,
    pre_f32,
    pre_send,
    pre_in,
    z_send,
    z_in,
    z_own,
    act,
    hid,
    out_send,
    out_in,
    rec,
    mate_in,
    fin_send,
    fin_in,
    fin_own,
    combine,
    moe_ref,
    row_own,
    row_mate,
    row_part,
    row_in,
    row_sum,
    row_zin,
    rows_dec,
    load_sem,
    tok_s,
    tok_r,
    mate_s,
    mate_r,
    gux_s,
    gux_r,
    guz_s,
    guz_r,
    hz_s,
    hz_r,
    hx_s,
    hx_r,
    px_s,
    px_r,
    pz_s,
    pz_r,
    az_s,
    az_r,
    ax_s,
    ax_r,
    out_s,
    out_r,
    cm_s,
    cm_r,
    fin_s,
    fin_r,
    rm_s,
    rm_r,
    ry_s,
    ry_r,
    rz_s,
    rz_r,
    rg_s,
    rg_r,
):
    e = lax.axis_index("exp")
    f = lax.axis_index("feat")
    chip, core = e // 2, e % 2
    y, zl = chip // 4, chip % 4
    zh, x = f // 4, f % 4
    mate = {"exp": chip * 2 + (1 - core), "feat": f}
    zpeer = {"exp": e, "feat": (1 - zh) * 4 + x}

    def xpeer(k):
        return {"exp": e, "feat": zh * 4 + (x + k) % 4}

    loads = [
        pltpu.make_async_copy(gate_hbm.at[0], gate_w, load_sem.at[0]),
        pltpu.make_async_copy(up_hbm.at[0], up_w, load_sem.at[1]),
        pltpu.make_async_copy(enc_hbm, enc_w, load_sem.at[2]),
        pltpu.make_async_copy(down_hbm.at[0], down_w, load_sem.at[3]),
        pltpu.make_async_copy(dec_hbm, dec_w.at[:, pl.ds(0, WIDTH)], load_sem.at[4]),
    ]
    for load in loads:
        load.start()

    barrier = pltpu.get_barrier_semaphore()

    def greet(k, carry):
        pl.semaphore_signal(
            barrier, inc=1, device_id={"exp": (e + k) % EXPERTS, "feat": f}, device_id_type=MESH
        )
        return carry

    lax.fori_loop(1, EXPERTS, greet, 0)
    for k in range(1, 4):
        pl.semaphore_signal(barrier, inc=1, device_id=xpeer(k), device_id_type=MESH)
    pl.semaphore_signal(barrier, inc=1, device_id=zpeer, device_id_type=MESH)
    lane = lax.broadcasted_iota(jnp.int32, (ROWS, EXTRA), 1)
    named = jnp.zeros((ROWS, EXTRA), F32)
    spread = jnp.zeros((ROWS, EXTRA), F32)
    for k in range(route_ref.shape[1]):
        hit = route_ref[:, k : k + 1] == lane
        named = jnp.where(hit, 1.0, named)
        spread = jnp.where(hit, weight_ref[:, k : k + 1], spread)
    earlier = jnp.where(
        lax.broadcasted_iota(jnp.int32, (ROWS, ROWS), 0)
        > lax.broadcasted_iota(jnp.int32, (ROWS, ROWS), 1),
        1.0,
        0.0,
    ).astype(BF16)
    before = dot(earlier, named.astype(BF16))
    code = jnp.where((named > 0) & (before < SLOT), before + 1.0, 0.0).astype(BF16)
    tok_all[e, :, pl.ds(0, WIDTH)] = tok_ref[...]
    tok_all[e, :, pl.ds(WIDTH, EXTRA)] = code
    pl.semaphore_wait(barrier, EXPERTS - 1 + 4)

    def token_copy(k):
        there = (chip + k) % CHIPS
        return remote(
            tok_all.at[e],
            tok_all.at[e],
            tok_s.at[k],
            tok_r.at[k],
            {"exp": there * 2 + core, "feat": f},
        )

    def token_pass(k):
        block = ((chip + CHIPS - k) % CHIPS) * 2 + core
        return remote(tok_all.at[block], tok_all.at[block], mate_s.at[k], mate_r.at[k], mate)

    def token_start(k, carry):
        token_copy(k).start()
        return carry

    lax.fori_loop(1, CHIPS, token_start, 0)
    token_pass(0).start()

    def token_forward(k, carry):
        token_copy(k).wait_recv()
        token_pass(k).start()
        return carry

    lax.fori_loop(1, CHIPS, token_forward, 0)

    slot_lane = lax.broadcasted_iota(jnp.int32, (EXTRA, EXPERTS * SLOT), 1)
    widen = jnp.where(
        (slot_lane >> 3) == lax.broadcasted_iota(jnp.int32, (EXTRA, EXPERTS * SLOT), 0), 1.0, 0.0
    ).astype(BF16)
    slot_wanted = (
        (lax.broadcasted_iota(jnp.int32, (ROWS, EXPERTS * SLOT), 1) & 7) + 1
    ).astype(F32)
    in_slot = dot(code, widen) == slot_wanted

    def three(value):
        high = value.astype(BF16)
        rest = value - high.astype(F32)
        middle = rest.astype(BF16)
        return high, middle, (rest - middle.astype(F32)).astype(BF16)

    for part, piece in enumerate(three(spread)):
        combine[part] = jnp.where(in_slot, dot(piece, widen), 0.0).astype(BF16)
    feature = lax.broadcasted_iota(jnp.int32, (FEATURES, EXTRA), 0) + e * FEATURES
    dec_w[:, pl.ds(WIDTH, EXTRA)] = jnp.where(feature == ids_ref[0:1, :], 1.0, 0.0).astype(BF16)

    def token_arrived(k, carry):
        token_pass(k).wait_recv()
        return carry

    lax.fori_loop(0, CHIPS, token_arrived, 0)

    everything = tok_all[...].reshape(EXPERTS * ROWS, WIDE)
    pick = jnp.where(lax.broadcasted_iota(jnp.int32, (8, EXTRA), 1) == e, 1.0, 0.0).astype(BF16)
    codes = lax.dot_general(
        pick, everything[:, WIDTH:], (((1,), (1,)), ((), ())), preferred_element_type=F32
    )
    slot_row = lax.broadcasted_iota(jnp.int32, (EXPERTS * SLOT, EXPERTS * ROWS), 0)
    token_col = lax.broadcasted_iota(jnp.int32, (EXPERTS * SLOT, EXPERTS * ROWS), 1)
    same_block = (slot_row >> 3) == (token_col >> 4)
    wanted = ((slot_row & 7) + 1).astype(F32)
    picker = jnp.where(same_block & (codes[0:1, :] == wanted), 1.0, 0.0).astype(BF16)
    expert_in = dot(picker, everything[:, :WIDTH]).astype(BF16)

    loads[0].wait()
    loads[1].wait()

    for half, weights in ((0, gate_w), (1, up_w)):

        def gate_tile(n, carry, half=half, weights=weights):
            at = pl.multiple_of(n * 256, 256)
            gu_own[:, pl.ds(pl.multiple_of(half * HIDDEN + n * 256, 256), 256)] = dot(
                expert_in, weights[:, pl.ds(at, 256)]
            )
            return carry

        lax.fori_loop(0, HIDDEN // 256, gate_tile, 0)

    def gux_copy(k):
        rows = pl.ds(((x + k) % 4) * 64, 64)
        return remote(gu_own.at[rows], gu_in.at[k - 1], gux_s.at[k - 1], gux_r.at[k - 1], xpeer(k))

    for k in (2, 1, 3):
        gux_copy(k).start()
    loads[2].wait()

    def blocks_of(j):
        return ((y + 1 + j) % 4) * 8

    def px_copy(j, k):
        rows = pl.ds(((x + k) % 4) * 32, 32)
        return remote(
            pre_send.at[j, rows], pre_in.at[j, k - 1], px_s.at[j, k - 1], px_r.at[j, k - 1], xpeer(k)
        )

    def pre_multiply(j):
        rows = tok_all[pl.ds(blocks_of(j), 8)].reshape(CHUNK_ROWS, WIDE)[:, :WIDTH]

        def tile(n, carry):
            at = pl.multiple_of(n * 256, 256)
            part = dot(rows, enc_w[:, pl.ds(at, 256)])
            pre_f32[j, :, pl.ds(at, 256)] = part
            pre_send[j, :, pl.ds(at, 256)] = part.astype(BF16)
            return carry

        lax.fori_loop(0, FEATURES // 256, tile, 0)
        for k in (2, 1, 3):
            px_copy(j, k).start()

    def pz_copy(j):
        return remote(z_send.at[j], z_in.at[j], pz_s.at[j], pz_r.at[j], zpeer)

    def pre_reduce(j):
        for k in (1, 3, 2):
            px_copy(j, k).wait_recv()
        for keep in (0, 1):
            first = (1 - zh if keep == 0 else zh) * 16
            total = pre_f32[j, pl.ds(pl.multiple_of(x * 32 + first, 16), 16), :]
            for k in range(3):
                total = total + pre_in[j, k, pl.ds(pl.multiple_of(first, 16), 16), :].astype(F32)
            if keep == 0:
                z_send[j] = total.astype(BF16)
                pz_copy(j).start()
            else:
                z_own[j] = total

    def owned(j):
        return blocks_of(j) + 2 * x + zh

    def passed(j):
        return blocks_of(j) + 2 * x + (1 - zh)

    def az_copy(j):
        return remote(act.at[owned(j)], act.at[owned(j)], az_s.at[j], az_r.at[j], zpeer)

    def ax_copy(j, k, second):
        block = passed(j) if second else owned(j)
        at = second * 3 + k - 1
        return remote(act.at[block], act.at[block], ax_s.at[j, at], ax_r.at[j, at], xpeer(k))

    def activate(j):
        pz_copy(j).wait_recv()
        pre = z_own[j] + z_in[j].astype(F32) + bias_ref[...]
        act[owned(j)] = jnp.maximum(pre, 0.0).astype(BF16)
        az_copy(j).start()
        for k in (2, 1, 3):
            ax_copy(j, k, 0).start()

    def pass_on(j):
        az_copy(j).wait_recv()
        for k in (2, 1, 3):
            ax_copy(j, k, 1).start()

    def guz_copy():
        return remote(gu_zsend, gu_zin, guz_s.at[0], guz_r.at[0], zpeer)

    def gu_reduce():
        for k in (1, 3, 2):
            gux_copy(k).wait_recv()
        for keep in (0, 1):
            first = (1 - zh if keep == 0 else zh) * 32
            mine = pl.ds(pl.multiple_of(x * 64 + first, 32), 32)
            total = gu_own[mine, :]
            for k in range(3):
                total = total + gu_in[k, pl.ds(pl.multiple_of(first, 32), 32), :]
            if keep == 0:
                gu_zsend[...] = total
                guz_copy().start()
            else:
                gu_own[mine, :] = total

    def hz_copy():
        return remote(hid.at[2 * x + zh], hid.at[2 * x + zh], hz_s.at[0], hz_r.at[0], zpeer)

    def hx_copy(k, second):
        part = 2 * x + ((1 - zh) if second else zh)
        at = second * 3 + k - 1
        return remote(hid.at[part], hid.at[part], hx_s.at[at], hx_r.at[at], xpeer(k))

    def gu_activate():
        guz_copy().wait_recv()
        mine = pl.ds(pl.multiple_of(x * 64 + zh * 32, 32), 32)
        total = gu_own[mine, :] + gu_zin[...]
        gate, up = total[:, :HIDDEN], total[:, HIDDEN:]
        hid[2 * x + zh] = (gate / (1.0 + jnp.exp(-gate)) * up).astype(BF16)
        hz_copy().start()
        for k in (2, 1, 3):
            hx_copy(k, 0).start()

    def gu_pass_on():
        hz_copy().wait_recv()
        for k in (2, 1, 3):
            hx_copy(k, 1).start()

    def out_copy(k):
        there = (e + k) % EXPERTS
        return remote(
            out_send.at[there],
            out_in.at[e],
            out_s.at[k],
            out_r.at[k],
            {"exp": there, "feat": f},
        )

    def down():
        for second in (0, 1):
            for k in (1, 3, 2):
                hx_copy(k, second).wait_recv()
        hidden = hid[...].reshape(EXPERTS * SLOT, HIDDEN)
        for n in range(7):
            cols = pl.ds(n * 128, 128)
            out_send[:, :, cols] = (
                dot(hidden, down_w[:, cols]).reshape(EXPERTS, SLOT, 128).astype(BF16)
            )
        out_in[e] = out_send[e]

        def start(k, carry):
            out_copy(k).start()
            return carry

        lax.fori_loop(1, EXPERTS, start, 0)

    def cm_copy(j):
        return remote(rec.at[j, 1 - core], mate_in.at[j], cm_s.at[j], cm_r.at[j], mate)

    def decode(j):
        for second in (0, 1):
            for k in (1, 3, 2):
                ax_copy(j, k, second).wait_recv()
        rows = act[pl.ds(blocks_of(j), 8)].reshape(CHUNK_ROWS, FEATURES)

        def tile(n, carry):
            at = pl.multiple_of(n * 256, 256)
            part = dot(rows, dec_w[:, pl.ds(at, 256)]).reshape(4, 2, ROWS, 256)
            for c in (0, 1):
                rec[j, c, :, :, pl.ds(at, 256)] = part[:, c]
            return carry

        lax.fori_loop(0, WIDE // 256, tile, 0)
        cm_copy(j).start()

    def fin_copy(j, k):
        there = ((y + 1 + j) % 4) * 4 + (zl + k) % 4
        at = ((1 + j) % 4) * 4 + k
        return remote(
            fin_send.at[j, k],
            fin_in.at[at],
            fin_s.at[at],
            fin_r.at[at],
            {"exp": there * 2 + core, "feat": f},
        )

    def finish(j):
        cm_copy(j).wait_recv()
        for k in range(4):
            to = (zl + k) % 4
            total = rec[j, core, to] + mate_in[j, to]
            if j == CHUNKS - 1 and k == 0:
                fin_own[...] = total
            else:
                fin_send[j, k] = total.astype(BF16)
                fin_copy(j, k).start()

    def row_mate_copy():
        return remote(row_own, row_mate, rm_s.at[0], rm_r.at[0], mate)

    def same_core(there_y, there_z):
        return {"exp": (there_y * 4 + there_z) * 2 + core, "feat": f}

    def row_y_copy(k):
        there = (y + k) % 4
        return remote(
            row_part.at[there], row_in.at[k - 1], ry_s.at[k - 1], ry_r.at[k - 1], same_core(there, zl)
        )

    def row_z_copy(k):
        return remote(
            row_sum, row_zin.at[k - 1], rz_s.at[k - 1], rz_r.at[k - 1], same_core(y, (zl + k) % 4)
        )

    def row_gather_copy(k):
        return remote(
            rows_dec.at[y], rows_dec.at[y], rg_s.at[k - 1], rg_r.at[k - 1], same_core((y + k) % 4, zl)
        )

    def rows_start():
        mine = lax.dot_general(
            dec_w[:, pl.ds(WIDTH, EXTRA)],
            dec_w[:, pl.ds(0, WIDTH)],
            (((0,), (0,)), ((), ())),
            preferred_element_type=F32,
        )
        row_own[...] = mine[:64].astype(BF16).reshape(4, ROWS, WIDTH)
        row_mate_copy().start()

    def rows_y():
        row_mate_copy().wait_recv()
        row_part[...] = (row_own[...].astype(F32) + row_mate[...].astype(F32)).astype(BF16)
        for k in range(1, 4):
            row_y_copy(k).start()

    def rows_z():
        total = row_part[y].astype(F32)
        for k in range(1, 4):
            row_y_copy(k).wait_recv()
            total = total + row_in[k - 1].astype(F32)
        row_sum[...] = total.astype(BF16)
        for k in range(1, 4):
            row_z_copy(k).start()

    def rows_gather():
        total = row_sum[...].astype(F32)
        for k in range(1, 4):
            row_z_copy(k).wait_recv()
            total = total + row_zin[k - 1].astype(F32)
        rows_dec[y] = total.astype(BF16)
        for k in range(1, 4):
            row_gather_copy(k).start()

    pre_multiply(0)
    pre_multiply(1)
    pre_multiply(2)
    pre_multiply(3)
    loads[4].wait()
    rows_start()
    gu_reduce()
    rows_y()
    pre_reduce(0)
    loads[3].wait()
    gu_activate()
    rows_z()
    pre_reduce(1)
    activate(0)
    gu_pass_on()
    pre_reduce(2)
    activate(1)
    pass_on(0)
    pre_reduce(3)
    rows_gather()
    down()
    activate(2)
    pass_on(1)
    decode(0)
    activate(3)
    pass_on(2)
    finish(0)
    decode(1)
    pass_on(3)
    finish(1)
    decode(2)

    def out_arrived(k, carry):
        out_copy(k).wait_recv()
        return carry

    lax.fori_loop(1, EXPERTS, out_arrived, 0)
    for n in range(7):
        cols = pl.ds(n * 128, 128)
        rows = out_in[:, :, cols].astype(F32).reshape(EXPERTS * SLOT, 128).astype(BF16)
        moe_ref[:, cols] = dot(combine[2], rows) + dot(combine[1], rows) + dot(combine[0], rows)
    finish(2)
    decode(3)
    finish(3)

    total = fin_own[...]
    for at in range(1, CHIPS):
        j, k = (at // 4 + 3) % 4, at % 4
        fin_copy(j, k).wait_recv()
        total = total + fin_in[at].astype(F32)
    err_ref[...] = moe_ref[...] - total[:, :WIDTH] - dbias_ref[...]
    for k in range(1, 4):
        row_gather_copy(k).wait_recv()
    change = values_ref[...].astype(F32) - total[:, WIDTH : WIDTH + 64]
    listed = rows_dec[...].reshape(64, WIDTH)
    high, middle, low = three(change)
    steered_ref[...] = moe_ref[...] + (dot(low, listed) + dot(middle, listed) + dot(high, listed))

    def tokens_left(k, carry):
        token_copy(k).wait_send()
        return carry

    lax.fori_loop(1, CHIPS, tokens_left, 0)

    def passes_left(k, carry):
        token_pass(k).wait_send()
        return carry

    lax.fori_loop(0, CHIPS, passes_left, 0)

    def outs_left(k, carry):
        out_copy(k).wait_send()
        return carry

    lax.fori_loop(1, EXPERTS, outs_left, 0)
    guz_copy().wait_send()
    hz_copy().wait_send()
    row_mate_copy().wait_send()
    for k in range(1, 4):
        row_y_copy(k).wait_send()
        row_z_copy(k).wait_send()
        row_gather_copy(k).wait_send()
        gux_copy(k).wait_send()
        hx_copy(k, 0).wait_send()
        hx_copy(k, 1).wait_send()
    for j in range(CHUNKS):
        pz_copy(j).wait_send()
        az_copy(j).wait_send()
        cm_copy(j).wait_send()
        for k in range(1, 4):
            px_copy(j, k).wait_send()
            ax_copy(j, k, 0).wait_send()
            ax_copy(j, k, 1).wait_send()
        for k in range(4):
            if not (j == CHUNKS - 1 and k == 0):
                fin_copy(j, k).wait_send()


def fused(*operands):
    vmem = pl.BlockSpec(memory_space=pltpu.VMEM)
    hbm = pl.BlockSpec(memory_space=pl.ANY)
    dma = pltpu.SemaphoreType.DMA
    scratch = [
        pltpu.VMEM((WIDTH, HIDDEN), BF16),
        pltpu.VMEM((WIDTH, HIDDEN), BF16),
        pltpu.VMEM((HIDDEN, WIDTH), BF16),
        pltpu.VMEM((WIDTH, FEATURES), BF16),
        pltpu.VMEM((FEATURES, WIDE), BF16),
        pltpu.VMEM((EXPERTS, ROWS, WIDE), BF16),
        pltpu.VMEM((EXPERTS * SLOT, 2 * HIDDEN), F32),
        pltpu.VMEM((3, 64, 2 * HIDDEN), F32),
        pltpu.VMEM((32, 2 * HIDDEN), F32),
        pltpu.VMEM((32, 2 * HIDDEN), F32),
        pltpu.VMEM((CHUNKS, CHUNK_ROWS, FEATURES), F32),
        pltpu.VMEM((CHUNKS, CHUNK_ROWS, FEATURES), BF16),
        pltpu.VMEM((CHUNKS, 3, 32, FEATURES), BF16),
        pltpu.VMEM((CHUNKS, ROWS, FEATURES), BF16),
        pltpu.VMEM((CHUNKS, ROWS, FEATURES), BF16),
        pltpu.VMEM((CHUNKS, ROWS, FEATURES), F32),
        pltpu.VMEM((EXPERTS, ROWS, FEATURES), BF16),
        pltpu.VMEM((8, 32, HIDDEN), BF16),
        pltpu.VMEM((EXPERTS, SLOT, WIDTH), BF16),
        pltpu.VMEM((EXPERTS, SLOT, WIDTH), BF16),
        pltpu.VMEM((CHUNKS, 2, 4, ROWS, WIDE), F32),
        pltpu.VMEM((CHUNKS, 4, ROWS, WIDE), F32),
        pltpu.VMEM((CHUNKS, 4, ROWS, WIDE), BF16),
        pltpu.VMEM((CHIPS, ROWS, WIDE), BF16),
        pltpu.VMEM((ROWS, WIDE), F32),
        pltpu.VMEM((3, ROWS, EXPERTS * SLOT), BF16),
        pltpu.VMEM((ROWS, WIDTH), F32),
        pltpu.VMEM((4, ROWS, WIDTH), BF16),
        pltpu.VMEM((4, ROWS, WIDTH), BF16),
        pltpu.VMEM((4, ROWS, WIDTH), BF16),
        pltpu.VMEM((3, ROWS, WIDTH), BF16),
        pltpu.VMEM((ROWS, WIDTH), BF16),
        pltpu.VMEM((3, ROWS, WIDTH), BF16),
        pltpu.VMEM((4, ROWS, WIDTH), BF16),
        dma((5,)),
        dma((CHIPS,)),
        dma((CHIPS,)),
        dma((CHIPS,)),
        dma((CHIPS,)),
        dma((3,)),
        dma((3,)),
        dma((1,)),
        dma((1,)),
        dma((1,)),
        dma((1,)),
        dma((6,)),
        dma((6,)),
        dma((CHUNKS, 3)),
        dma((CHUNKS, 3)),
        dma((CHUNKS,)),
        dma((CHUNKS,)),
        dma((CHUNKS,)),
        dma((CHUNKS,)),
        dma((CHUNKS, 6)),
        dma((CHUNKS, 6)),
        dma((EXPERTS,)),
        dma((EXPERTS,)),
        dma((CHUNKS,)),
        dma((CHUNKS,)),
        dma((CHIPS,)),
        dma((CHIPS,)),
        dma((1,)),
        dma((1,)),
        dma((3,)),
        dma((3,)),
        dma((3,)),
        dma((3,)),
        dma((3,)),
        dma((3,)),
    ]
    return pl.pallas_call(
        kernel,
        out_shape=(
            jax.ShapeDtypeStruct((ROWS, WIDTH), F32),
            jax.ShapeDtypeStruct((ROWS, WIDTH), F32),
        ),
        in_specs=[vmem] * 7 + [hbm] * 5,
        out_specs=(vmem, vmem),
        scratch_shapes=scratch,
        name="fused_layer",
        cost_estimate=pl.CostEstimate(
            flops=6_000_000_000, bytes_accessed=400_000_000, transcendentals=0
        ),
        compiler_params=pltpu.CompilerParams(
            collective_id=0, has_side_effects=True, vmem_limit_bytes=56 << 20
        ),
    )(*operands)


def local(
    tokens,
    route_ids,
    route_weights,
    gate_proj,
    up_proj,
    down_proj,
    enc_weight,
    enc_bias,
    dec_weight,
    dec_bias,
    clamp_ids,
    clamp_values,
):
    ids = jnp.pad(clamp_ids, (0, EXTRA - clamp_ids.shape[0]), constant_values=-1)
    return fused(
        tokens,
        route_ids,
        route_weights,
        enc_bias[None, :],
        dec_bias[None, :],
        ids[None, :],
        clamp_values[None, :],
        gate_proj,
        up_proj,
        down_proj,
        enc_weight,
        dec_weight,
    )


def solution(mesh):
    placed = (
        P("exp", "feat"),
        P("exp", None),
        P("exp", None),
        P("exp", "feat", None),
        P("exp", "feat", None),
        P("exp", None, "feat"),
        P("feat", "exp"),
        P("exp"),
        P("exp", "feat"),
        P("feat"),
        P(),
        P(),
    )
    return jax.shard_map(
        local,
        mesh=mesh,
        in_specs=placed,
        out_specs=(P("exp", "feat"), P("exp", "feat")),
        check_vma=False,
    )
```

```python
import functools

import jax
import jax.numpy as jnp
from jax import lax
from jax.experimental import pallas as pl
from jax.experimental.pallas import tpu as pltpu
from jax.sharding import PartitionSpec as P

SLOT = 8
ROWS = 16
WIDTH = 896
EXTRA = 128
WIDE = WIDTH + EXTRA
FEATURES = 2048
HIDDEN = 1024
CHIPS = 16
EXPERTS = 32
CHUNKS = 4
CHUNK_ROWS = 128
MESH = pl.DeviceIdType.MESH
F32 = jnp.float32
BF16 = jnp.bfloat16


def remote(src, dst, send_sem, recv_sem, device):
    return pltpu.make_async_remote_copy(
        src_ref=src,
        dst_ref=dst,
        send_sem=send_sem,
        recv_sem=recv_sem,
        device_id=device,
        device_id_type=MESH,
    )


def dot(a, b):
    return jnp.dot(a, b, preferred_element_type=F32)


def kernel(
    tok_ref,
    route_ref,
    weight_ref,
    bias_ref,
    ids_ref,
    values_ref,
    gate_hbm,
    up_hbm,
    down_hbm,
    enc_hbm,
    dec_hbm,
    recon_ref,
    moe_ref,
    shift_ref,
    gate_w,
    up_w,
    down_w,
    enc_w,
    dec_w,
    tok_all,
    gu_own,
    gu_ring,
    gu_in,
    gu_zsend,
    gu_zin,
    pre_f32,
    pre_send,
    pre_ring,
    pre_in,
    z_send,
    z_in,
    z_own,
    act,
    hid,
    out_send,
    out_in,
    rec,
    mate_in,
    fin_send,
    fin_in,
    fin_own,
    combine,
    row_own,
    row_mate,
    row_part,
    row_in,
    row_sum,
    row_zin,
    rows_dec,
    load_sem,
    tz_s,
    tz_r,
    ty_s,
    ty_r,
    mate_s,
    mate_r,
    gux_s,
    gux_r,
    guz_s,
    guz_r,
    hz_s,
    hz_r,
    hx_s,
    hx_r,
    px_s,
    px_r,
    pz_s,
    pz_r,
    az_s,
    az_r,
    ax_s,
    ax_r,
    out_s,
    out_r,
    cm_s,
    cm_r,
    fin_s,
    fin_r,
    rm_s,
    rm_r,
    ry_s,
    ry_r,
    rz_s,
    rz_r,
    rg_s,
    rg_r,
):
    e = lax.axis_index("exp")
    f = lax.axis_index("feat")
    chip, core = e // 2, e % 2
    y, zl = chip // 4, chip % 4
    zh, x = f // 4, f % 4
    mate = {"exp": chip * 2 + (1 - core), "feat": f}
    zpeer = {"exp": e, "feat": (1 - zh) * 4 + x}

    def xpeer(k):
        return {"exp": e, "feat": zh * 4 + (x + k) % 4}

    load_enc = pltpu.make_async_copy(enc_hbm, enc_w, load_sem.at[0])
    load_gate = pltpu.make_async_copy(gate_hbm.at[0], gate_w, load_sem.at[1])
    load_up = pltpu.make_async_copy(up_hbm.at[0], up_w, load_sem.at[2])
    load_dec = pltpu.make_async_copy(dec_hbm, dec_w.at[:, pl.ds(0, WIDTH)], load_sem.at[3])
    load_down = pltpu.make_async_copy(down_hbm.at[0], down_w, load_sem.at[4])
    for load in (load_enc, load_gate, load_up, load_dec, load_down):
        load.start()

    barrier = pltpu.get_barrier_semaphore()

    def greet(k, carry):
        pl.semaphore_signal(
            barrier, inc=1, device_id={"exp": (e + k) % EXPERTS, "feat": f}, device_id_type=MESH
        )
        return carry

    lax.fori_loop(1, EXPERTS, greet, 0)
    for k in range(1, 4):
        pl.semaphore_signal(barrier, inc=1, device_id=xpeer(k), device_id_type=MESH)
    pl.semaphore_signal(barrier, inc=1, device_id=zpeer, device_id_type=MESH)
    expert_of = lax.broadcasted_iota(jnp.int32, (EXTRA, ROWS), 0)
    named = jnp.zeros((EXTRA, ROWS), F32)
    spread = jnp.zeros((EXTRA, ROWS), F32)
    for k in range(route_ref.shape[0]):
        hit = route_ref[k : k + 1, :] == expert_of
        named = jnp.where(hit, 1.0, named)
        spread = jnp.where(hit, weight_ref[k : k + 1, :], spread)
    one = lax.broadcasted_iota(jnp.int32, (ROWS, ROWS), 0)
    other = lax.broadcasted_iota(jnp.int32, (ROWS, ROWS), 1)
    before = dot(named.astype(BF16), jnp.where(one < other, 1.0, 0.0).astype(BF16))
    code_t = jnp.where((named > 0) & (before < SLOT), before + 1.0, 0.0).astype(BF16)
    code = lax.dot_general(
        jnp.where(one == other, 1.0, 0.0).astype(BF16),
        code_t,
        (((1,), (1,)), ((), ())),
        preferred_element_type=F32,
    ).astype(BF16)
    tok_all[e, :, pl.ds(0, WIDTH)] = tok_ref[...]
    tok_all[e, :, pl.ds(WIDTH, EXTRA)] = code
    pl.semaphore_wait(barrier, EXPERTS - 1 + 4)

    def same_core(there_y, there_z):
        return {"exp": (there_y * 4 + there_z) * 2 + core, "feat": f}

    def block_at(back_y, back_z, which):
        return (((y + 4 - back_y) % 4) * 4 + (zl + 4 - back_z) % 4) * 2 + which

    def token_z(k):
        return remote(
            tok_all.at[e], tok_all.at[e], tz_s.at[k - 1], tz_r.at[k - 1], same_core(y, (zl + k) % 4)
        )

    def token_z_arrival(k):
        block = block_at(0, k, core)
        return remote(tok_all.at[block], tok_all.at[block], tz_s.at[k - 1], tz_r.at[k - 1], mate)

    def token_y(k, m):
        block = block_at(0, m, core)
        at = (k - 1) * 4 + m
        return remote(
            tok_all.at[block], tok_all.at[block], ty_s.at[at], ty_r.at[at], same_core((y + k) % 4, zl)
        )

    def token_y_arrival(k, m):
        block = block_at(k, m, core)
        at = (k - 1) * 4 + m
        return remote(tok_all.at[block], tok_all.at[block], ty_s.at[at], ty_r.at[at], mate)

    def token_pass(k, m):
        block = block_at(k, m, core)
        at = k * 4 + m
        return remote(tok_all.at[block], tok_all.at[block], mate_s.at[at], mate_r.at[at], mate)

    def token_pass_arrival(k, m):
        block = block_at(k, m, 1 - core)
        at = k * 4 + m
        return remote(tok_all.at[block], tok_all.at[block], mate_s.at[at], mate_r.at[at], mate)

    for k in (1, 3, 2):
        token_z(k).start()
    token_pass(0, 0).start()
    for k in (2, 1, 3):
        token_y(k, 0).start()
    for m in (1, 3, 2):
        token_z_arrival(m).wait_recv()
        token_pass(0, m).start()
        for k in (2, 1, 3):
            token_y(k, m).start()

    def from_y(k):
        for m in (0, 1, 3, 2):
            token_y_arrival(k, m).wait_recv()
            token_pass(k, m).start()

    def from_mate(k):
        for m in (0, 1, 3, 2):
            token_pass_arrival(k, m).wait_recv()

    slot_lane = lax.broadcasted_iota(jnp.int32, (EXTRA, EXPERTS * SLOT), 1)
    widen = jnp.where(
        (slot_lane >> 3) == lax.broadcasted_iota(jnp.int32, (EXTRA, EXPERTS * SLOT), 0), 1.0, 0.0
    ).astype(BF16)
    slot_wanted = (
        (lax.broadcasted_iota(jnp.int32, (ROWS, EXPERTS * SLOT), 1) & 7) + 1
    ).astype(F32)
    in_slot = dot(code, widen) == slot_wanted

    def three(value):
        high = value.astype(BF16)
        rest = value - high.astype(F32)
        middle = rest.astype(BF16)
        return high, middle, (rest - middle.astype(F32)).astype(BF16)

    for part, piece in enumerate(three(spread)):
        widened = lax.dot_general(
            piece, widen, (((0,), (0,)), ((), ())), preferred_element_type=F32
        )
        combine[part] = jnp.where(in_slot, widened, 0.0).astype(BF16)
    clamps = ids_ref.shape[1]
    feature = lax.broadcasted_iota(jnp.int32, (FEATURES, clamps), 0) + e * FEATURES
    listed_col = jnp.where(feature == ids_ref[...], 1.0, 0.0).astype(BF16)
    dec_w[:, pl.ds(WIDTH, EXTRA)] = jnp.concatenate(
        [listed_col, jnp.zeros((FEATURES, EXTRA - clamps), BF16)], axis=1
    )

    toward = (1, 3)

    def quarter(k):
        return (x + k) % 4

    def half_rows(k, half, size):
        return pl.ds(pl.multiple_of(quarter(k) * 2 * size + half * size, size), size)

    def gu_ring_copy(n):
        return remote(
            gu_own.at[half_rows(2, n, 32)],
            gu_ring.at[n],
            gux_s.at[n],
            gux_r.at[n],
            xpeer(toward[n]),
        )

    def gu_early(n):
        return remote(
            gu_own.at[half_rows(toward[n], 1 - n, 32)],
            gu_in.at[1 - n, 0],
            gux_s.at[2 + n],
            gux_r.at[2 + n],
            xpeer(toward[n]),
        )

    def gu_late(n):
        return remote(
            gu_own.at[half_rows(toward[n], n, 32)],
            gu_in.at[n, 1],
            gux_s.at[4 + n],
            gux_r.at[4 + n],
            xpeer(toward[n]),
        )

    def gu_relay():
        for n in (0, 1):
            gu_ring_copy(n).wait_recv()
            rows = half_rows(toward[n], n, 32)
            gu_own[rows, :] = gu_own[rows, :] + gu_ring[n]
            gu_late(n).start()

    def gu_multiply():
        everything = tok_all[...].reshape(EXPERTS * ROWS, WIDE)
        pick = jnp.where(lax.broadcasted_iota(jnp.int32, (8, EXTRA), 1) == e, 1.0, 0.0).astype(BF16)
        codes = lax.dot_general(
            pick, everything[:, WIDTH:], (((1,), (1,)), ((), ())), preferred_element_type=F32
        )
        slot_row = lax.broadcasted_iota(jnp.int32, (EXPERTS * SLOT, EXPERTS * ROWS), 0)
        token_col = lax.broadcasted_iota(jnp.int32, (EXPERTS * SLOT, EXPERTS * ROWS), 1)
        same_block = (slot_row >> 3) == (token_col >> 4)
        wanted = ((slot_row & 7) + 1).astype(F32)
        picker = jnp.where(same_block & (codes[0:1, :] == wanted), 1.0, 0.0).astype(BF16)
        expert_in = dot(picker, everything[:, :WIDTH]).astype(BF16)

        load_gate.wait()
        load_up.wait()
        for half, weights in ((0, gate_w), (1, up_w)):

            def gate_tile(n, carry, half=half, weights=weights):
                at = pl.multiple_of(n * 256, 256)
                gu_own[:, pl.ds(pl.multiple_of(half * HIDDEN + n * 256, 256), 256)] = dot(
                    expert_in, weights[:, pl.ds(at, 256)]
                )
                return carry

            lax.fori_loop(0, HIDDEN // 256, gate_tile, 0)
        for n in (0, 1):
            gu_ring_copy(n).start()
        for n in (0, 1):
            gu_early(n).start()

    def blocks_of(j):
        return ((y + j) % 4) * 8

    def pre_ring_copy(j, n):
        return remote(
            pre_send.at[j, half_rows(2, n, 16)],
            pre_ring.at[j, n],
            px_s.at[j, n],
            px_r.at[j, n],
            xpeer(toward[n]),
        )

    def pre_early(j, n):
        return remote(
            pre_send.at[j, half_rows(toward[n], 1 - n, 16)],
            pre_in.at[j, 1 - n, 0],
            px_s.at[j, 2 + n],
            px_r.at[j, 2 + n],
            xpeer(toward[n]),
        )

    def pre_late(j, n):
        return remote(
            pre_send.at[j, half_rows(toward[n], n, 16)],
            pre_in.at[j, n, 1],
            px_s.at[j, 4 + n],
            px_r.at[j, 4 + n],
            xpeer(toward[n]),
        )

    def pre_relay(j):
        for n in (0, 1):
            pre_ring_copy(j, n).wait_recv()
            rows = half_rows(toward[n], n, 16)
            pre_send[j, rows, :] = (pre_f32[j, rows, :] + pre_ring[j, n].astype(F32)).astype(BF16)
            pre_late(j, n).start()

    def pre_multiply(j):
        rows = tok_all[pl.ds(blocks_of(j), 8)].reshape(CHUNK_ROWS, WIDE)[:, :WIDTH]

        def tile(n, carry):
            at = pl.multiple_of(n * 256, 256)
            part = dot(rows, enc_w[:, pl.ds(at, 256)])
            pre_f32[j, :, pl.ds(at, 256)] = part
            pre_send[j, :, pl.ds(at, 256)] = part.astype(BF16)
            return carry

        lax.fori_loop(0, FEATURES // 256, tile, 0)
        for n in (0, 1):
            pre_ring_copy(j, n).start()
        for n in (0, 1):
            pre_early(j, n).start()

    def pz_copy(j):
        return remote(z_send.at[j], z_in.at[j], pz_s.at[j], pz_r.at[j], zpeer)

    def pre_reduce(j):
        for n in (0, 1):
            pre_early(j, n).wait_recv()
            pre_late(j, n).wait_recv()
        for keep in (0, 1):
            half = 1 - zh if keep == 0 else zh
            total = pre_f32[j, half_rows(0, half, 16), :]
            for k in range(2):
                total = total + pre_in[j, half, k].astype(F32)
            if keep == 0:
                z_send[j] = total.astype(BF16)
                pz_copy(j).start()
            else:
                z_own[j] = total

    def owned(j):
        return blocks_of(j) + 2 * x + zh

    def passed(j):
        return blocks_of(j) + 2 * x + (1 - zh)

    def az_copy(j):
        return remote(act.at[owned(j)], act.at[owned(j)], az_s.at[j], az_r.at[j], zpeer)

    def block_of(j, k, side):
        return blocks_of(j) + 2 * quarter(k) + side

    def ax_copy(j, n, second):
        block = passed(j) if second else owned(j)
        at = second * 2 + n
        return remote(act.at[block], act.at[block], ax_s.at[j, at], ax_r.at[j, at], xpeer(toward[n]))

    def ax_relay(j, n):
        block = block_of(j, toward[1 - n], zh if n == 0 else 1 - zh)
        return remote(
            act.at[block], act.at[block], ax_s.at[j, 4 + n], ax_r.at[j, 4 + n], xpeer(toward[n])
        )

    def activate(j):
        pz_copy(j).wait_recv()
        pre = z_own[j] + z_in[j].astype(F32) + bias_ref[...]
        act[owned(j)] = jnp.maximum(pre, 0.0).astype(BF16)
        az_copy(j).start()
        for n in (0, 1):
            ax_copy(j, n, 0).start()

    def pass_on(j):
        az_copy(j).wait_recv()
        for n in (1, 0):
            ax_copy(j, n, 1).start()

    def relay(j):
        ax_copy(j, 0, 0).wait_recv()
        ax_relay(j, 0).start()
        ax_copy(j, 1, 1).wait_recv()
        ax_relay(j, 1).start()

    def guz_copy():
        return remote(gu_zsend, gu_zin, guz_s.at[0], guz_r.at[0], zpeer)

    def gu_reduce():
        for n in (0, 1):
            gu_early(n).wait_recv()
            gu_late(n).wait_recv()
        for keep in (0, 1):
            half = 1 - zh if keep == 0 else zh
            mine = half_rows(0, half, 32)
            total = gu_own[mine, :] + gu_in[half, 0] + gu_in[half, 1]
            if keep == 0:
                gu_zsend[...] = total
                guz_copy().start()
            else:
                gu_own[mine, :] = total

    def hz_copy():
        return remote(hid.at[2 * x + zh], hid.at[2 * x + zh], hz_s.at[0], hz_r.at[0], zpeer)

    def hx_copy(n, second):
        part = 2 * x + ((1 - zh) if second else zh)
        at = second * 2 + n
        return remote(hid.at[part], hid.at[part], hx_s.at[at], hx_r.at[at], xpeer(toward[n]))

    def hx_relay(n):
        part = 2 * quarter(toward[1 - n]) + (zh if n == 0 else 1 - zh)
        return remote(hid.at[part], hid.at[part], hx_s.at[4 + n], hx_r.at[4 + n], xpeer(toward[n]))

    def gu_activate():
        guz_copy().wait_recv()
        total = gu_own[half_rows(0, zh, 32), :] + gu_zin[...]
        gate, up = total[:, :HIDDEN], total[:, HIDDEN:]
        hid[2 * x + zh] = (gate / (1.0 + jnp.exp(-gate)) * up).astype(BF16)
        hz_copy().start()
        for n in (0, 1):
            hx_copy(n, 0).start()

    def gu_pass_on():
        hz_copy().wait_recv()
        for n in (1, 0):
            hx_copy(n, 1).start()

    def hid_relay():
        hx_copy(0, 0).wait_recv()
        hx_relay(0).start()
        hx_copy(1, 1).wait_recv()
        hx_relay(1).start()

    def out_copy(k):
        there = (e + k) % EXPERTS
        return remote(
            out_send.at[there],
            out_in.at[e],
            out_s.at[k],
            out_r.at[k],
            {"exp": there, "feat": f},
        )

    def down():
        hx_copy(1, 0).wait_recv()
        hx_copy(0, 1).wait_recv()
        hx_relay(0).wait_recv()
        hx_relay(1).wait_recv()
        load_down.wait()
        hidden = hid[...].reshape(EXPERTS * SLOT, HIDDEN)
        for n in range(7):
            cols = pl.ds(n * 128, 128)
            out_send[:, :, cols] = (
                dot(hidden, down_w[:, cols]).reshape(EXPERTS, SLOT, 128).astype(BF16)
            )
        out_in[e] = out_send[e]

        def start(k, carry):
            out_copy(k).start()
            return carry

        lax.fori_loop(1, EXPERTS, start, 0)

    def cm_copy(j):
        return remote(rec.at[j, 1 - core], mate_in.at[j], cm_s.at[j], cm_r.at[j], mate)

    def decode(j):
        ax_copy(j, 1, 0).wait_recv()
        ax_copy(j, 0, 1).wait_recv()
        ax_relay(j, 0).wait_recv()
        ax_relay(j, 1).wait_recv()
        rows = act[pl.ds(blocks_of(j), 8)].reshape(CHUNK_ROWS, FEATURES)

        def tile(n, carry):
            at = pl.multiple_of(n * 256, 256)
            part = dot(rows, dec_w[:, pl.ds(at, 256)]).reshape(4, 2, ROWS, 256)
            for c in (0, 1):
                rec[j, c, :, :, pl.ds(at, 256)] = part[:, c]
            return carry

        lax.fori_loop(0, WIDE // 256, tile, 0)
        cm_copy(j).start()

    def fin_copy(j, k):
        there = ((y + j) % 4) * 4 + (zl + k) % 4
        at = j * 4 + k
        return remote(
            fin_send.at[j, k],
            fin_in.at[at],
            fin_s.at[at],
            fin_r.at[at],
            {"exp": there * 2 + core, "feat": f},
        )

    def finish(j):
        cm_copy(j).wait_recv()
        for k in range(4):
            to = (zl + k) % 4
            total = rec[j, core, to] + mate_in[j, to]
            if j == 0 and k == 0:
                fin_own[...] = total
            else:
                fin_send[j, k] = total.astype(BF16)
                fin_copy(j, k).start()

    def row_mate_copy():
        return remote(row_own, row_mate, rm_s.at[0], rm_r.at[0], mate)

    def row_y_copy(k):
        there = (y + k) % 4
        return remote(
            row_part.at[there], row_in.at[k - 1], ry_s.at[k - 1], ry_r.at[k - 1], same_core(there, zl)
        )

    def row_z_copy(k):
        return remote(
            row_sum, row_zin.at[k - 1], rz_s.at[k - 1], rz_r.at[k - 1], same_core(y, (zl + k) % 4)
        )

    def row_gather_copy(k):
        return remote(
            rows_dec.at[y], rows_dec.at[y], rg_s.at[k - 1], rg_r.at[k - 1], same_core((y + k) % 4, zl)
        )

    def rows_start():
        mine = lax.dot_general(
            dec_w[:, pl.ds(WIDTH, EXTRA)],
            dec_w[:, pl.ds(0, WIDTH)],
            (((0,), (0,)), ((), ())),
            preferred_element_type=F32,
        )
        row_own[...] = mine[:64].astype(BF16).reshape(4, ROWS, WIDTH)
        row_mate_copy().start()

    def rows_y():
        row_mate_copy().wait_recv()
        row_part[...] = (row_own[...].astype(F32) + row_mate[...].astype(F32)).astype(BF16)
        for k in range(1, 4):
            row_y_copy(k).start()

    def rows_z():
        total = row_part[y].astype(F32)
        for k in range(1, 4):
            row_y_copy(k).wait_recv()
            total = total + row_in[k - 1].astype(F32)
        row_sum[...] = total.astype(BF16)
        for k in range(1, 4):
            row_z_copy(k).start()

    def rows_gather():
        total = row_sum[...].astype(F32)
        for k in range(1, 4):
            row_z_copy(k).wait_recv()
            total = total + row_zin[k - 1].astype(F32)
        rows_dec[y] = total.astype(BF16)
        for k in range(1, 4):
            row_gather_copy(k).start()

    from_mate(0)
    load_enc.wait()
    pre_multiply(0)
    for k in (1, 3, 2):
        from_y(k)
    for k in (1, 3, 2):
        from_mate(k)
    gu_multiply()
    pre_relay(0)
    pre_multiply(1)
    pre_reduce(0)
    pre_multiply(2)
    activate(0)
    pre_multiply(3)
    pass_on(0)
    load_dec.wait()
    rows_start()
    gu_relay()
    relay(0)
    pre_relay(1)
    rows_y()
    gu_reduce()
    pre_reduce(1)
    pre_relay(2)
    gu_activate()
    activate(1)
    rows_z()
    pre_reduce(2)
    gu_pass_on()
    pass_on(1)
    pre_relay(3)
    activate(2)
    hid_relay()
    relay(1)
    pre_reduce(3)
    rows_gather()
    pass_on(2)
    down()
    decode(0)
    activate(3)
    finish(0)
    relay(2)
    pass_on(3)
    decode(1)
    finish(1)
    relay(3)
    decode(2)
    finish(2)

    def out_arrived(k, carry):
        out_copy(k).wait_recv()
        return carry

    lax.fori_loop(1, EXPERTS, out_arrived, 0)
    for n in range(7):
        cols = pl.ds(n * 128, 128)
        rows = out_in[:, :, cols].astype(F32).reshape(EXPERTS * SLOT, 128).astype(BF16)
        moe_ref[:, cols] = dot(combine[2], rows) + dot(combine[1], rows) + dot(combine[0], rows)
    decode(3)
    finish(3)

    total = fin_own[...]
    for at in range(1, CHIPS):
        j, k = at // 4, at % 4
        fin_copy(j, k).wait_recv()
        total = total + fin_in[at].astype(F32)
    recon_ref[...] = total[:, :WIDTH]
    for k in range(1, 4):
        row_gather_copy(k).wait_recv()
    change = values_ref[...].astype(F32) - total[:, WIDTH : WIDTH + clamps]
    listed = rows_dec[...].reshape(64, WIDTH)
    high, middle, low = three(change)
    shift_ref[...] = dot(low, listed) + dot(middle, listed) + dot(high, listed)

    for k in range(1, 4):
        token_z(k).wait_send()
        for m in range(4):
            token_y(k, m).wait_send()
    for k in range(4):
        for m in range(4):
            token_pass(k, m).wait_send()

    def outs_left(k, carry):
        out_copy(k).wait_send()
        return carry

    lax.fori_loop(1, EXPERTS, outs_left, 0)
    guz_copy().wait_send()
    hz_copy().wait_send()
    row_mate_copy().wait_send()
    for k in range(1, 4):
        row_y_copy(k).wait_send()
        row_z_copy(k).wait_send()
        row_gather_copy(k).wait_send()
    for n in (0, 1):
        gu_ring_copy(n).wait_send()
        gu_early(n).wait_send()
        gu_late(n).wait_send()
        hx_copy(n, 0).wait_send()
        hx_copy(n, 1).wait_send()
        hx_relay(n).wait_send()
    for j in range(CHUNKS):
        pz_copy(j).wait_send()
        az_copy(j).wait_send()
        cm_copy(j).wait_send()
        for n in (0, 1):
            pre_ring_copy(j, n).wait_send()
            pre_early(j, n).wait_send()
            pre_late(j, n).wait_send()
            ax_copy(j, n, 0).wait_send()
            ax_copy(j, n, 1).wait_send()
            ax_relay(j, n).wait_send()
        for k in range(4):
            if not (j == 0 and k == 0):
                fin_copy(j, k).wait_send()


def fused(*operands):
    vmem = pl.BlockSpec(memory_space=pltpu.VMEM)
    hbm = pl.BlockSpec(memory_space=pl.ANY)
    dma = pltpu.SemaphoreType.DMA
    scratch = [
        pltpu.VMEM((WIDTH, HIDDEN), BF16),
        pltpu.VMEM((WIDTH, HIDDEN), BF16),
        pltpu.VMEM((HIDDEN, WIDTH), BF16),
        pltpu.VMEM((WIDTH, FEATURES), BF16),
        pltpu.VMEM((FEATURES, WIDE), BF16),
        pltpu.VMEM((EXPERTS, ROWS, WIDE), BF16),
        pltpu.VMEM((EXPERTS * SLOT, 2 * HIDDEN), F32),
        pltpu.VMEM((2, 32, 2 * HIDDEN), F32),
        pltpu.VMEM((2, 2, 32, 2 * HIDDEN), F32),
        pltpu.VMEM((32, 2 * HIDDEN), F32),
        pltpu.VMEM((32, 2 * HIDDEN), F32),
        pltpu.VMEM((CHUNKS, CHUNK_ROWS, FEATURES), F32),
        pltpu.VMEM((CHUNKS, CHUNK_ROWS, FEATURES), BF16),
        pltpu.VMEM((CHUNKS, 2, ROWS, FEATURES), BF16),
        pltpu.VMEM((CHUNKS, 2, 2, ROWS, FEATURES), BF16),
        pltpu.VMEM((CHUNKS, ROWS, FEATURES), BF16),
        pltpu.VMEM((CHUNKS, ROWS, FEATURES), BF16),
        pltpu.VMEM((CHUNKS, ROWS, FEATURES), F32),
        pltpu.VMEM((EXPERTS, ROWS, FEATURES), BF16),
        pltpu.VMEM((8, 32, HIDDEN), BF16),
        pltpu.VMEM((EXPERTS, SLOT, WIDTH), BF16),
        pltpu.VMEM((EXPERTS, SLOT, WIDTH), BF16),
        pltpu.VMEM((CHUNKS, 2, 4, ROWS, WIDE), F32),
        pltpu.VMEM((CHUNKS, 4, ROWS, WIDE), F32),
        pltpu.VMEM((CHUNKS, 4, ROWS, WIDE), BF16),
        pltpu.VMEM((CHIPS, ROWS, WIDE), BF16),
        pltpu.VMEM((ROWS, WIDE), F32),
        pltpu.VMEM((3, ROWS, EXPERTS * SLOT), BF16),
        pltpu.VMEM((4, ROWS, WIDTH), BF16),
        pltpu.VMEM((4, ROWS, WIDTH), BF16),
        pltpu.VMEM((4, ROWS, WIDTH), BF16),
        pltpu.VMEM((3, ROWS, WIDTH), BF16),
        pltpu.VMEM((ROWS, WIDTH), BF16),
        pltpu.VMEM((3, ROWS, WIDTH), BF16),
        pltpu.VMEM((4, ROWS, WIDTH), BF16),
        dma((5,)),
        dma((3,)),
        dma((3,)),
        dma((12,)),
        dma((12,)),
        dma((CHIPS,)),
        dma((CHIPS,)),
        dma((6,)),
        dma((6,)),
        dma((1,)),
        dma((1,)),
        dma((1,)),
        dma((1,)),
        dma((6,)),
        dma((6,)),
        dma((CHUNKS, 6)),
        dma((CHUNKS, 6)),
        dma((CHUNKS,)),
        dma((CHUNKS,)),
        dma((CHUNKS,)),
        dma((CHUNKS,)),
        dma((CHUNKS, 6)),
        dma((CHUNKS, 6)),
        dma((EXPERTS,)),
        dma((EXPERTS,)),
        dma((CHUNKS,)),
        dma((CHUNKS,)),
        dma((CHIPS,)),
        dma((CHIPS,)),
        dma((1,)),
        dma((1,)),
        dma((3,)),
        dma((3,)),
        dma((3,)),
        dma((3,)),
        dma((3,)),
        dma((3,)),
    ]
    return pl.pallas_call(
        kernel,
        out_shape=(
            jax.ShapeDtypeStruct((ROWS, WIDTH), F32),
            jax.ShapeDtypeStruct((ROWS, WIDTH), F32),
            jax.ShapeDtypeStruct((ROWS, WIDTH), F32),
        ),
        in_specs=[vmem] * 6 + [hbm] * 5,
        out_specs=(vmem, vmem, vmem),
        scratch_shapes=scratch,
        name="fused_layer",
        cost_estimate=pl.CostEstimate(
            flops=6_000_000_000, bytes_accessed=400_000_000, transcendentals=0
        ),
        compiler_params=pltpu.CompilerParams(
            collective_id=0, has_side_effects=True, vmem_limit_bytes=56 << 20
        ),
    )(*operands)


def local(
    tokens,
    route_ids,
    route_weights,
    gate_proj,
    up_proj,
    down_proj,
    enc_weight,
    enc_bias,
    dec_weight,
    dec_bias,
    clamp_ids,
    clamp_values,
):
    recon, moe_out, shift = fused(
        tokens,
        route_ids.T,
        route_weights.T,
        enc_bias[None, :],
        clamp_ids[None, :],
        clamp_values[None, :],
        gate_proj,
        up_proj,
        down_proj,
        enc_weight,
        dec_weight,
    )
    return moe_out - recon - dec_bias, moe_out + shift


def solution(mesh):
    placed = (
        P("exp", "feat"),
        P("exp", None),
        P("exp", None),
        P("exp", "feat", None),
        P("exp", "feat", None),
        P("exp", None, "feat"),
        P("feat", "exp"),
        P("exp"),
        P("exp", "feat"),
        P("feat"),
        P(),
        P(),
    )
    return jax.shard_map(
        local,
        mesh=mesh,
        in_specs=placed,
        out_specs=(P("exp", "feat"), P("exp", "feat")),
        check_vma=False,
    )
```

```python
import functools

import jax
import jax.numpy as jnp
from jax import lax
from jax.experimental import pallas as pl
from jax.experimental.pallas import tpu as pltpu
from jax.sharding import PartitionSpec as P

SLOT = 8
ROWS = 16
WIDTH = 896
EXTRA = 128
WIDE = WIDTH + EXTRA
FEATURES = 2048
HIDDEN = 1024
CHIPS = 16
EXPERTS = 32
CHUNKS = 4
CHUNK_ROWS = 128
MESH = pl.DeviceIdType.MESH
F32 = jnp.float32
BF16 = jnp.bfloat16


def remote(src, dst, send_sem, recv_sem, device):
    return pltpu.make_async_remote_copy(
        src_ref=src,
        dst_ref=dst,
        send_sem=send_sem,
        recv_sem=recv_sem,
        device_id=device,
        device_id_type=MESH,
    )


def dot(a, b):
    return jnp.dot(a, b, preferred_element_type=F32)


def kernel(
    tok_hbm,
    route_hbm,
    weight_hbm,
    bias_hbm,
    ids_hbm,
    values_hbm,
    gate_hbm,
    up_hbm,
    down_hbm,
    enc_hbm,
    dec_hbm,
    recon_hbm,
    moe_hbm,
    shift_hbm,
    route_ref,
    weight_ref,
    bias_ref,
    ids_ref,
    values_ref,
    recon_ref,
    moe_ref,
    shift_ref,
    expert_in,
    gate_w,
    up_w,
    down_w,
    enc_w,
    dec_w,
    tok_all,
    gu_own,
    gu_ring,
    gu_in,
    gu_zsend,
    gu_zin,
    pre_f32,
    pre_send,
    pre_ring,
    pre_in,
    z_send,
    z_in,
    z_own,
    act,
    hid,
    out_send,
    out_in,
    rec,
    mate_in,
    fin_send,
    fin_in,
    fin_own,
    combine,
    row_own,
    row_mate,
    row_part,
    row_in,
    row_sum,
    row_zin,
    rows_dec,
    load_sem,
    sent,
    tz_r,
    ty_r,
    mate_r,
    gux_r,
    guz_r,
    hz_r,
    hx_r,
    px_r,
    pz_r,
    az_r,
    ax_r,
    out_r,
    cm_r,
    fin_r,
    rm_r,
    ry_r,
    rz_r,
    rg_r,
):
    e = lax.axis_index("exp")
    f = lax.axis_index("feat")
    chip, core = e // 2, e % 2
    y, zl = chip // 4, chip % 4
    zh, x = f // 4, f % 4
    mate = {"exp": chip * 2 + (1 - core), "feat": f}
    zpeer = {"exp": e, "feat": (1 - zh) * 4 + x}

    def xpeer(k):
        return {"exp": e, "feat": zh * 4 + (x + k) % 4}

    load_enc = pltpu.make_async_copy(enc_hbm, enc_w, load_sem.at[0])
    load_gate = pltpu.make_async_copy(gate_hbm.at[0], gate_w, load_sem.at[1])
    load_up = pltpu.make_async_copy(up_hbm.at[0], up_w, load_sem.at[2])
    load_dec = pltpu.make_async_copy(dec_hbm, dec_w.at[:, pl.ds(0, WIDTH)], load_sem.at[3])
    load_down = pltpu.make_async_copy(down_hbm.at[0], down_w, load_sem.at[4])
    small = [
        pltpu.make_async_copy(source, target, load_sem.at[5 + n])
        for n, (source, target) in enumerate(
            (
                (route_hbm, route_ref),
                (weight_hbm, weight_ref),
                (tok_hbm, tok_all.at[e, :, pl.ds(0, WIDTH)]),
                (ids_hbm, ids_ref),
                (values_hbm, values_ref),
                (bias_hbm, bias_ref),
            )
        )
    ]
    for load in small:
        load.start()
    for load in (load_enc, load_gate, load_up, load_dec, load_down):
        load.start()

    barrier = pltpu.get_barrier_semaphore()

    def greet(k, carry):
        pl.semaphore_signal(
            barrier, inc=1, device_id={"exp": (e + k) % EXPERTS, "feat": f}, device_id_type=MESH
        )
        return carry

    lax.fori_loop(1, EXPERTS, greet, 0)
    for k in (1, 3):
        pl.semaphore_signal(barrier, inc=1, device_id=xpeer(k), device_id_type=MESH)
    pl.semaphore_signal(barrier, inc=1, device_id=zpeer, device_id_type=MESH)
    small[0].wait()
    small[1].wait()
    expert_of = lax.broadcasted_iota(jnp.int32, (EXTRA, ROWS), 0)
    named = jnp.zeros((EXTRA, ROWS), F32)
    spread = jnp.zeros((EXTRA, ROWS), F32)
    for k in range(route_ref.shape[0]):
        hit = route_ref[k : k + 1, :] == expert_of
        named = jnp.where(hit, 1.0, named)
        spread = jnp.where(hit, weight_ref[k : k + 1, :], spread)
    one = lax.broadcasted_iota(jnp.int32, (ROWS, ROWS), 0)
    other = lax.broadcasted_iota(jnp.int32, (ROWS, ROWS), 1)
    before = dot(named.astype(BF16), jnp.where(one < other, 1.0, 0.0).astype(BF16))
    code_t = jnp.where((named > 0) & (before < SLOT), before + 1.0, 0.0).astype(BF16)
    code = lax.dot_general(
        jnp.where(one == other, 1.0, 0.0).astype(BF16),
        code_t,
        (((1,), (1,)), ((), ())),
        preferred_element_type=F32,
    ).astype(BF16)
    small[2].wait()
    tok_all[e, :, pl.ds(WIDTH, EXTRA)] = code
    pl.semaphore_wait(barrier, EXPERTS - 1 + 3)

    def same_core(there_y, there_z):
        return {"exp": (there_y * 4 + there_z) * 2 + core, "feat": f}

    def block_at(back_y, back_z, which):
        return (((y + 4 - back_y) % 4) * 4 + (zl + 4 - back_z) % 4) * 2 + which

    def token_z(k):
        return remote(
            tok_all.at[e], tok_all.at[e], sent.at[0], tz_r.at[k - 1], same_core(y, (zl + k) % 4)
        )

    def token_z_arrival(k):
        block = block_at(0, k, core)
        return remote(tok_all.at[block], tok_all.at[block], sent.at[0], tz_r.at[k - 1], mate)

    def token_y(k, m):
        block = block_at(0, m, core)
        at = (k - 1) * 4 + m
        return remote(
            tok_all.at[block], tok_all.at[block], sent.at[0], ty_r.at[at], same_core((y + k) % 4, zl)
        )

    def token_y_arrival(k, m):
        block = block_at(k, m, core)
        at = (k - 1) * 4 + m
        return remote(tok_all.at[block], tok_all.at[block], sent.at[0], ty_r.at[at], mate)

    def token_pass(k, m):
        block = block_at(k, m, core)
        return remote(tok_all.at[block], tok_all.at[block], sent.at[0], mate_r.at[k], mate)

    def four_passed(k):
        four = tok_all.at[pl.ds(0, 4)]
        return remote(four, four, sent.at[0], mate_r.at[k], mate)

    for k in (1, 3, 2):
        token_z(k).start()
    token_pass(0, 0).start()
    for k in (2, 1, 3):
        token_y(k, 0).start()
    for m in (1, 3, 2):
        token_z_arrival(m).wait_recv()
        token_pass(0, m).start()
        for k in (2, 1, 3):
            token_y(k, m).start()

    def from_y(k):
        for m in (0, 1, 3, 2):
            token_y_arrival(k, m).wait_recv()
            token_pass(k, m).start()

    def from_mate(k):
        four_passed(k).wait_recv()

    clamps = ids_ref.shape[1]

    def three(value):
        high = value.astype(BF16)
        rest = value - high.astype(F32)
        middle = rest.astype(BF16)
        return high, middle, (rest - middle.astype(F32)).astype(BF16)

    def route_weights():
        slot_lane = lax.broadcasted_iota(jnp.int32, (EXTRA, EXPERTS * SLOT), 1)
        widen = jnp.where(
            (slot_lane >> 3) == lax.broadcasted_iota(jnp.int32, (EXTRA, EXPERTS * SLOT), 0), 1.0, 0.0
        ).astype(BF16)
        slot_wanted = (
            (lax.broadcasted_iota(jnp.int32, (ROWS, EXPERTS * SLOT), 1) & 7) + 1
        ).astype(F32)
        in_slot = dot(code, widen) == slot_wanted

        for part, piece in enumerate(three(spread)):
            widened = lax.dot_general(
                piece, widen, (((0,), (0,)), ((), ())), preferred_element_type=F32
            )
            combine[part] = jnp.where(in_slot, widened, 0.0).astype(BF16)

    def listed_columns():
        small[3].wait()
        feature = lax.broadcasted_iota(jnp.int32, (FEATURES, clamps), 0) + e * FEATURES
        listed_col = jnp.where(feature == ids_ref[...], 1.0, 0.0).astype(BF16)
        dec_w[:, pl.ds(WIDTH, EXTRA)] = jnp.concatenate(
            [listed_col, jnp.zeros((FEATURES, EXTRA - clamps), BF16)], axis=1
        )

    toward = (1, 3)

    def quarter(k):
        return (x + k) % 4

    def half_rows(k, half, size):
        return pl.ds(pl.multiple_of(quarter(k) * 2 * size + half * size, size), size)

    def gu_rows(h, k, half):
        return pl.ds(pl.multiple_of(h * 128 + quarter(k) * 32 + half * 16, 16), 16)

    def gu_ring_copy(h, n):
        return remote(
            gu_own.at[gu_rows(h, 2, n)],
            gu_ring.at[h, n],
            sent.at[1],
            gux_r.at[h, n],
            xpeer(toward[n]),
        )

    def gu_early(h, n):
        return remote(
            gu_own.at[gu_rows(h, toward[n], 1 - n)],
            gu_in.at[h, 1 - n, 0],
            sent.at[1],
            gux_r.at[h, 2],
            xpeer(toward[n]),
        )

    def gu_late(h, n):
        return remote(
            gu_own.at[gu_rows(h, toward[n], n)],
            gu_in.at[h, n, 1],
            sent.at[1],
            gux_r.at[h, 2],
            xpeer(toward[n]),
        )

    def gu_relay(h):
        for n in (0, 1):
            gu_ring_copy(h, n).wait_recv()
            rows = gu_rows(h, toward[n], n)
            gu_own[rows, :] = gu_own[rows, :] + gu_ring[h, n]
            gu_late(h, n).start()

    def gu_pick():
        everything = tok_all[...].reshape(EXPERTS * ROWS, WIDE)
        pick = jnp.where(lax.broadcasted_iota(jnp.int32, (8, EXTRA), 1) == e, 1.0, 0.0).astype(BF16)
        codes = lax.dot_general(
            pick, everything[:, WIDTH:], (((1,), (1,)), ((), ())), preferred_element_type=F32
        )
        slot_row = lax.broadcasted_iota(jnp.int32, (EXPERTS * SLOT, EXPERTS * ROWS), 0)
        token_col = lax.broadcasted_iota(jnp.int32, (EXPERTS * SLOT, EXPERTS * ROWS), 1)
        same_block = (((slot_row >> 3) + e) & (EXPERTS - 1)) == (token_col >> 4)
        wanted = ((slot_row & 7) + 1).astype(F32)
        picker = jnp.where(same_block & (codes[0:1, :] == wanted), 1.0, 0.0).astype(BF16)
        expert_in[...] = dot(picker, everything[:, :WIDTH]).astype(BF16)
        load_gate.wait()
        load_up.wait()

    def gu_multiply(h):
        rows = pl.ds(h * 128, 128)
        for half, weights in ((0, gate_w), (1, up_w)):

            def gate_tile(n, carry, half=half, weights=weights):
                at = pl.multiple_of(n * 256, 256)
                gu_own[rows, pl.ds(pl.multiple_of(half * HIDDEN + n * 256, 256), 256)] = dot(
                    expert_in[rows, :], weights[:, pl.ds(at, 256)]
                )
                return carry

            lax.fori_loop(0, HIDDEN // 256, gate_tile, 0)
        for n in (0, 1):
            gu_ring_copy(h, n).start()
        for n in (0, 1):
            gu_early(h, n).start()

    def blocks_of(j):
        return ((y + j) % 4) * 8

    def pre_ring_copy(j, n):
        return remote(
            pre_send.at[j, half_rows(2, n, 16)],
            pre_ring.at[j, n],
            sent.at[2],
            px_r.at[j, n],
            xpeer(toward[n]),
        )

    def pre_early(j, n):
        return remote(
            pre_send.at[j, half_rows(toward[n], 1 - n, 16)],
            pre_in.at[j, 1 - n, 0],
            sent.at[2],
            px_r.at[j, 2],
            xpeer(toward[n]),
        )

    def pre_late(j, n):
        return remote(
            pre_send.at[j, half_rows(toward[n], n, 16)],
            pre_in.at[j, n, 1],
            sent.at[2],
            px_r.at[j, 2],
            xpeer(toward[n]),
        )

    def pre_relay(j):
        for n in (0, 1):
            pre_ring_copy(j, n).wait_recv()
            rows = half_rows(toward[n], n, 16)
            pre_send[j, rows, :] = (pre_f32[j, rows, :] + pre_ring[j, n].astype(F32)).astype(BF16)
            pre_late(j, n).start()

    def pre_multiply(j):
        rows = tok_all[pl.ds(blocks_of(j), 8)].reshape(CHUNK_ROWS, WIDE)[:, :WIDTH]

        def tile(n, carry):
            at = pl.multiple_of(n * 256, 256)
            part = dot(rows, enc_w[:, pl.ds(at, 256)])
            pre_f32[j, :, pl.ds(at, 256)] = part
            pre_send[j, :, pl.ds(at, 256)] = part.astype(BF16)
            return carry

        lax.fori_loop(0, FEATURES // 256, tile, 0)
        for n in (0, 1):
            pre_ring_copy(j, n).start()
        for n in (0, 1):
            pre_early(j, n).start()

    def pz_copy(j):
        return remote(z_send.at[j], z_in.at[j], sent.at[2], pz_r.at[j], zpeer)

    def pre_reduce(j):
        remote(pre_in.at[j], pre_in.at[j], sent.at[2], px_r.at[j, 2], mate).wait_recv()
        for keep in (0, 1):
            half = 1 - zh if keep == 0 else zh
            total = pre_f32[j, half_rows(0, half, 16), :]
            for k in range(2):
                total = total + pre_in[j, half, k].astype(F32)
            if keep == 0:
                z_send[j] = total.astype(BF16)
                pz_copy(j).start()
            else:
                z_own[j] = total

    def owned(j):
        return blocks_of(j) + 2 * x + zh

    def passed(j):
        return blocks_of(j) + 2 * x + (1 - zh)

    def az_copy(j):
        return remote(act.at[owned(j)], act.at[owned(j)], sent.at[3], az_r.at[j], zpeer)

    def block_of(j, k, side):
        return blocks_of(j) + 2 * quarter(k) + side

    def ax_copy(j, n, second):
        block = passed(j) if second else owned(j)
        at = n if n == second else 2
        return remote(act.at[block], act.at[block], sent.at[3], ax_r.at[j, at], xpeer(toward[n]))

    def ax_relay(j, n):
        block = block_of(j, toward[1 - n], zh if n == 0 else 1 - zh)
        return remote(
            act.at[block], act.at[block], sent.at[3], ax_r.at[j, 2], xpeer(toward[n])
        )

    def activate(j):
        pz_copy(j).wait_recv()
        if j == 0:
            small[5].wait()
        pre = z_own[j] + z_in[j].astype(F32) + bias_ref[...]
        act[owned(j)] = jnp.maximum(pre, 0.0).astype(BF16)
        az_copy(j).start()
        for n in (0, 1):
            ax_copy(j, n, 0).start()

    def pass_on(j):
        az_copy(j).wait_recv()
        for n in (1, 0):
            ax_copy(j, n, 1).start()

    def relay(j):
        ax_copy(j, 0, 0).wait_recv()
        ax_relay(j, 0).start()
        ax_copy(j, 1, 1).wait_recv()
        ax_relay(j, 1).start()

    def guz_copy(h):
        return remote(gu_zsend.at[h], gu_zin.at[h], sent.at[1], guz_r.at[h], zpeer)

    def gu_reduce(h):
        remote(gu_in.at[h], gu_in.at[h], sent.at[1], gux_r.at[h, 2], mate).wait_recv()
        for keep in (0, 1):
            half = 1 - zh if keep == 0 else zh
            mine = gu_rows(h, 0, half)
            total = gu_own[mine, :] + gu_in[h, half, 0] + gu_in[h, half, 1]
            if keep == 0:
                gu_zsend[h] = total
                guz_copy(h).start()
            else:
                gu_own[mine, :] = total

    def hid_of(h, k, side):
        return h * 8 + 2 * quarter(k) + side

    def hz_copy(h):
        part = hid_of(h, 0, zh)
        return remote(hid.at[part], hid.at[part], sent.at[4], hz_r.at[h], zpeer)

    def hx_copy(h, n, second):
        part = hid_of(h, 0, (1 - zh) if second else zh)
        at = n if n == second else 2
        return remote(hid.at[part], hid.at[part], sent.at[4], hx_r.at[h, at], xpeer(toward[n]))

    def hx_relay(h, n):
        part = hid_of(h, toward[1 - n], zh if n == 0 else 1 - zh)
        return remote(hid.at[part], hid.at[part], sent.at[4], hx_r.at[h, 2], xpeer(toward[n]))

    def gu_activate(h):
        guz_copy(h).wait_recv()
        total = gu_own[gu_rows(h, 0, zh), :] + gu_zin[h]
        gate, up = total[:, :HIDDEN], total[:, HIDDEN:]
        hid[hid_of(h, 0, zh)] = (gate / (1.0 + jnp.exp(-gate)) * up).astype(BF16)
        hz_copy(h).start()
        for n in (0, 1):
            hx_copy(h, n, 0).start()

    def gu_pass_on(h):
        hz_copy(h).wait_recv()
        for n in (1, 0):
            hx_copy(h, n, 1).start()

    def hid_relay(h):
        hx_copy(h, 0, 0).wait_recv()
        hx_relay(h, 0).start()
        hx_copy(h, 1, 1).wait_recv()
        hx_relay(h, 1).start()

    def out_copy(k):
        there = (e + k) % EXPERTS
        return remote(
            out_send.at[k], out_in.at[e], sent.at[5], out_r.at[0], {"exp": there, "feat": f}
        )

    def down(h):
        four = hid.at[pl.ds(0, 4)]
        remote(four, four, sent.at[4], hx_r.at[h, 2], mate).wait_recv()
        if h == 0:
            load_down.wait()
        hidden = hid[pl.ds(h * 8, 8)].reshape(128, HIDDEN)
        for n in range(7):
            cols = pl.ds(n * 128, 128)
            out_send[pl.ds(h * 16, 16), :, cols] = (
                dot(hidden, down_w[:, cols]).reshape(16, SLOT, 128).astype(BF16)
            )
        if h == 0:
            out_in[e] = out_send[0]

        def start(k, carry):
            out_copy(k).start()
            return carry

        lax.fori_loop(1 if h == 0 else 16, h * 16 + 16, start, 0)

    def cm_copy(j):
        return remote(rec.at[j, 1 - core], mate_in.at[j], sent.at[6], cm_r.at[j], mate)

    def decode(j):
        four = act.at[pl.ds(0, 4)]
        remote(four, four, sent.at[3], ax_r.at[j, 2], mate).wait_recv()
        rows = act[pl.ds(blocks_of(j), 8)].reshape(CHUNK_ROWS, FEATURES)

        def tile(n, carry):
            at = pl.multiple_of(n * 256, 256)
            part = dot(rows, dec_w[:, pl.ds(at, 256)]).reshape(4, 2, ROWS, 256)
            for c in (0, 1):
                rec[j, c, :, :, pl.ds(at, 256)] = part[:, c]
            return carry

        lax.fori_loop(0, WIDE // 256, tile, 0)
        cm_copy(j).start()

    def fin_copy(j, k):
        there = ((y + j) % 4) * 4 + (zl + k) % 4
        at = j * 4 + k
        return remote(
            fin_send.at[j, k],
            fin_in.at[at],
            sent.at[7],
            fin_r.at[0],
            {"exp": there * 2 + core, "feat": f},
        )

    def finish(j):
        cm_copy(j).wait_recv()
        for k in range(4):
            to = (zl + k) % 4
            total = rec[j, core, to] + mate_in[j, to]
            if j == 0 and k == 0:
                fin_own[...] = total
            else:
                fin_send[j, k] = total.astype(BF16)
                fin_copy(j, k).start()

    def row_mate_copy():
        return remote(row_own, row_mate, sent.at[8], rm_r.at[0], mate)

    def row_y_copy(k):
        there = (y + k) % 4
        return remote(
            row_part.at[there], row_in.at[k - 1], sent.at[8], ry_r.at[k - 1], same_core(there, zl)
        )

    def row_z_copy(k):
        return remote(
            row_sum, row_zin.at[k - 1], sent.at[8], rz_r.at[k - 1], same_core(y, (zl + k) % 4)
        )

    def row_gather_copy(k):
        return remote(
            rows_dec.at[y], rows_dec.at[y], sent.at[8], rg_r.at[k - 1], same_core((y + k) % 4, zl)
        )

    def rows_start():
        mine = lax.dot_general(
            dec_w[:, pl.ds(WIDTH, EXTRA)],
            dec_w[:, pl.ds(0, WIDTH)],
            (((0,), (0,)), ((), ())),
            preferred_element_type=F32,
        )
        row_own[...] = mine[:64].astype(BF16).reshape(4, ROWS, WIDTH)
        row_mate_copy().start()

    def rows_y():
        row_mate_copy().wait_recv()
        row_part[...] = (row_own[...].astype(F32) + row_mate[...].astype(F32)).astype(BF16)
        for k in range(1, 4):
            row_y_copy(k).start()

    def rows_z():
        total = row_part[y].astype(F32)
        for k in range(1, 4):
            row_y_copy(k).wait_recv()
            total = total + row_in[k - 1].astype(F32)
        row_sum[...] = total.astype(BF16)
        for k in range(1, 4):
            row_z_copy(k).start()

    def rows_gather():
        total = row_sum[...].astype(F32)
        for k in range(1, 4):
            row_z_copy(k).wait_recv()
            total = total + row_zin[k - 1].astype(F32)
        rows_dec[y] = total.astype(BF16)
        for k in range(1, 4):
            row_gather_copy(k).start()

    def combine_moe():
        most = out_in.at[pl.ds(1, EXPERTS - 1)]
        remote(most, most, sent.at[5], out_r.at[0], mate).wait_recv()
        for n in range(7):
            cols = pl.ds(n * 128, 128)
            rows = out_in[:, :, cols].astype(F32).reshape(EXPERTS * SLOT, 128).astype(BF16)
            moe_ref[:, cols] = dot(combine[2], rows) + dot(combine[1], rows) + dot(combine[0], rows)
        write_moe.start()

    def total_up():
        most = fin_in.at[pl.ds(1, CHIPS - 1)]
        remote(most, most, sent.at[7], fin_r.at[0], mate).wait_recv()
        total = fin_own[...]
        for at in range(1, CHIPS):
            total = total + fin_in[at].astype(F32)
        recon_ref[...] = total[:, :WIDTH]
        write_recon.start()
        for k in range(1, 4):
            row_gather_copy(k).wait_recv()
        small[4].wait()
        change = values_ref[...].astype(F32) - total[:, WIDTH : WIDTH + clamps]
        listed = rows_dec[...].reshape(64, WIDTH)
        high, middle, low = three(change)
        shift_ref[...] = dot(low, listed) + dot(middle, listed) + dot(high, listed)
        write_shift.start()

    write_recon = pltpu.make_async_copy(recon_ref, recon_hbm, load_sem.at[11])
    write_moe = pltpu.make_async_copy(moe_ref, moe_hbm, load_sem.at[12])
    write_shift = pltpu.make_async_copy(shift_ref, shift_hbm, load_sem.at[13])

    from_mate(0)
    load_enc.wait()
    pre_multiply(0)
    for k in (1, 3, 2):
        from_y(k)
    for k in (1, 3, 2):
        from_mate(k)
    pre_relay(0)
    pre_multiply(1)
    pre_multiply(2)
    pre_reduce(0)
    gu_pick()
    gu_multiply(0)
    pre_relay(1)
    route_weights()
    pre_multiply(3)
    load_dec.wait()
    listed_columns()
    rows_start()
    activate(0)
    pre_relay(2)
    gu_multiply(1)
    pre_reduce(1)
    rows_y()
    pre_relay(3)
    pre_reduce(2)
    rows_z()
    gu_relay(0)
    pass_on(0)
    rows_gather()
    activate(1)
    pre_reduce(3)
    gu_relay(1)
    activate(2)
    gu_reduce(0)
    relay(0)
    pass_on(1)
    activate(3)
    pass_on(2)
    gu_reduce(1)
    gu_activate(0)
    decode(0)
    pass_on(3)
    relay(1)
    relay(2)
    finish(0)
    gu_pass_on(0)
    relay(3)
    decode(1)
    gu_activate(1)
    finish(1)
    hid_relay(0)
    decode(2)
    gu_pass_on(1)
    finish(2)
    down(0)
    decode(3)
    hid_relay(1)
    finish(3)
    down(1)
    total_up()
    combine_moe()

    for kind, ref in (
        (0, tok_all.at[pl.ds(0, 31)]),
        (1, gu_own.at[pl.ds(0, 224)]),
        (2, act.at[pl.ds(0, 28)]),
        (3, act.at[pl.ds(0, 28)]),
        (4, hid.at[pl.ds(0, 14)]),
        (5, out_send.at[pl.ds(1, 31)]),
        (6, mate_in),
        (7, fin_in.at[pl.ds(1, 15)]),
        (8, out_send.at[pl.ds(0, 26)]),
    ):
        remote(ref, ref, sent.at[kind], rm_r.at[0], mate).wait_send()
    for write in (write_recon, write_moe, write_shift):
        write.wait()


def fused(*operands):
    hbm = pl.BlockSpec(memory_space=pl.ANY)
    dma = pltpu.SemaphoreType.DMA
    scratch = [
        pltpu.VMEM((8, ROWS), jnp.int32),
        pltpu.VMEM((8, ROWS), F32),
        pltpu.VMEM((1, FEATURES), F32),
        pltpu.VMEM(operands[4].shape, jnp.int32),
        pltpu.VMEM(operands[5].shape, BF16),
        pltpu.VMEM((ROWS, WIDTH), F32),
        pltpu.VMEM((ROWS, WIDTH), F32),
        pltpu.VMEM((ROWS, WIDTH), F32),
        pltpu.VMEM((EXPERTS * SLOT, WIDTH), BF16),
        pltpu.VMEM((WIDTH, HIDDEN), BF16),
        pltpu.VMEM((WIDTH, HIDDEN), BF16),
        pltpu.VMEM((HIDDEN, WIDTH), BF16),
        pltpu.VMEM((WIDTH, FEATURES), BF16),
        pltpu.VMEM((FEATURES, WIDE), BF16),
        pltpu.VMEM((EXPERTS, ROWS, WIDE), BF16),
        pltpu.VMEM((EXPERTS * SLOT, 2 * HIDDEN), F32),
        pltpu.VMEM((2, 2, ROWS, 2 * HIDDEN), F32),
        pltpu.VMEM((2, 2, 2, ROWS, 2 * HIDDEN), F32),
        pltpu.VMEM((2, ROWS, 2 * HIDDEN), F32),
        pltpu.VMEM((2, ROWS, 2 * HIDDEN), F32),
        pltpu.VMEM((CHUNKS, CHUNK_ROWS, FEATURES), F32),
        pltpu.VMEM((CHUNKS, CHUNK_ROWS, FEATURES), BF16),
        pltpu.VMEM((CHUNKS, 2, ROWS, FEATURES), BF16),
        pltpu.VMEM((CHUNKS, 2, 2, ROWS, FEATURES), BF16),
        pltpu.VMEM((CHUNKS, ROWS, FEATURES), BF16),
        pltpu.VMEM((CHUNKS, ROWS, FEATURES), BF16),
        pltpu.VMEM((CHUNKS, ROWS, FEATURES), F32),
        pltpu.VMEM((EXPERTS, ROWS, FEATURES), BF16),
        pltpu.VMEM((2 * 8, ROWS, HIDDEN), BF16),
        pltpu.VMEM((EXPERTS, SLOT, WIDTH), BF16),
        pltpu.VMEM((EXPERTS, SLOT, WIDTH), BF16),
        pltpu.VMEM((CHUNKS, 2, 4, ROWS, WIDE), F32),
        pltpu.VMEM((CHUNKS, 4, ROWS, WIDE), F32),
        pltpu.VMEM((CHUNKS, 4, ROWS, WIDE), BF16),
        pltpu.VMEM((CHIPS, ROWS, WIDE), BF16),
        pltpu.VMEM((ROWS, WIDE), F32),
        pltpu.VMEM((3, ROWS, EXPERTS * SLOT), BF16),
        pltpu.VMEM((4, ROWS, WIDTH), BF16),
        pltpu.VMEM((4, ROWS, WIDTH), BF16),
        pltpu.VMEM((4, ROWS, WIDTH), BF16),
        pltpu.VMEM((3, ROWS, WIDTH), BF16),
        pltpu.VMEM((ROWS, WIDTH), BF16),
        pltpu.VMEM((3, ROWS, WIDTH), BF16),
        pltpu.VMEM((4, ROWS, WIDTH), BF16),
        dma((14,)),
        dma((9,)),
        dma((3,)),
        dma((12,)),
        dma((4,)),
        dma((2, 3)),
        dma((2,)),
        dma((2,)),
        dma((2, 3)),
        dma((CHUNKS, 3)),
        dma((CHUNKS,)),
        dma((CHUNKS,)),
        dma((CHUNKS, 3)),
        dma((1,)),
        dma((CHUNKS,)),
        dma((1,)),
        dma((1,)),
        dma((3,)),
        dma((3,)),
        dma((3,)),
    ]
    return pl.pallas_call(
        kernel,
        out_shape=(
            jax.ShapeDtypeStruct((ROWS, WIDTH), F32),
            jax.ShapeDtypeStruct((ROWS, WIDTH), F32),
            jax.ShapeDtypeStruct((ROWS, WIDTH), F32),
        ),
        in_specs=[hbm] * 11,
        out_specs=(hbm, hbm, hbm),
        scratch_shapes=scratch,
        name="fused_layer",
        cost_estimate=pl.CostEstimate(
            flops=6_000_000_000, bytes_accessed=400_000_000, transcendentals=0
        ),
        compiler_params=pltpu.CompilerParams(
            collective_id=0, has_side_effects=True, vmem_limit_bytes=56 << 20
        ),
    )(*operands)


def local(
    tokens,
    route_ids,
    route_weights,
    gate_proj,
    up_proj,
    down_proj,
    enc_weight,
    enc_bias,
    dec_weight,
    dec_bias,
    clamp_ids,
    clamp_values,
):
    recon, moe_out, shift = fused(
        tokens,
        route_ids.T,
        route_weights.T,
        enc_bias[None, :],
        clamp_ids[None, :],
        clamp_values[None, :],
        gate_proj,
        up_proj,
        down_proj,
        enc_weight,
        dec_weight,
    )
    return moe_out - recon - dec_bias, moe_out + shift


def solution(mesh):
    placed = (
        P("exp", "feat"),
        P("exp", None),
        P("exp", None),
        P("exp", "feat", None),
        P("exp", "feat", None),
        P("exp", None, "feat"),
        P("feat", "exp"),
        P("exp"),
        P("exp", "feat"),
        P("feat"),
        P(),
        P(),
    )
    return jax.shard_map(
        local,
        mesh=mesh,
        in_specs=placed,
        out_specs=(P("exp", "feat"), P("exp", "feat")),
        check_vma=False,
    )
```

```python
import functools

import jax
import jax.numpy as jnp
from jax import lax
from jax.experimental import pallas as pl
from jax.experimental.pallas import tpu as pltpu
from jax.sharding import PartitionSpec as P

SLOT = 8
ROWS = 16
WIDTH = 896
EXTRA = 128
WIDE = WIDTH + EXTRA
FEATURES = 2048
HIDDEN = 1024
CHIPS = 16
EXPERTS = 32
CHUNKS = 4
CHUNK_ROWS = 128
MESH = pl.DeviceIdType.MESH
F32 = jnp.float32
BF16 = jnp.bfloat16


def remote(src, dst, send_sem, recv_sem, device):
    return pltpu.make_async_remote_copy(
        src_ref=src,
        dst_ref=dst,
        send_sem=send_sem,
        recv_sem=recv_sem,
        device_id=device,
        device_id_type=MESH,
    )


def dot(a, b):
    return jnp.dot(a, b, preferred_element_type=F32)


def kernel(
    tok_hbm,
    route_hbm,
    weight_hbm,
    bias_hbm,
    ids_hbm,
    values_hbm,
    gate_hbm,
    up_hbm,
    down_hbm,
    enc_hbm,
    dec_hbm,
    recon_hbm,
    moe_hbm,
    shift_hbm,
    route_ref,
    weight_ref,
    bias_ref,
    ids_ref,
    values_ref,
    recon_ref,
    moe_ref,
    shift_ref,
    expert_in,
    gate_w,
    up_w,
    down_w,
    enc_w,
    dec_w,
    tok_all,
    gu_own,
    gu_ring,
    gu_in,
    gu_zsend,
    gu_zin,
    pre_f32,
    pre_send,
    pre_ring,
    pre_in,
    z_send,
    z_in,
    z_own,
    act,
    hid,
    out_send,
    out_in,
    rec,
    mate_in,
    fin_send,
    fin_in,
    fin_own,
    fin_zsend,
    fin_zin,
    combine,
    row_own,
    row_mate,
    row_part,
    row_in,
    row_sum,
    row_zin,
    rows_dec,
    load_sem,
    sent,
    tz_r,
    ty_r,
    mate_r,
    gux_r,
    guz_r,
    hz_r,
    hx_r,
    px_r,
    pz_r,
    ax_r,
    out_r,
    cm_r,
    fin_r,
    rm_r,
    ry_r,
    rz_r,
    rg_r,
):
    e = lax.axis_index("exp")
    f = lax.axis_index("feat")
    chip, core = e // 2, e % 2
    y, zl = chip // 4, chip % 4
    zh, x = f // 4, f % 4
    mate = {"exp": chip * 2 + (1 - core), "feat": f}
    zpeer = {"exp": e, "feat": (1 - zh) * 4 + x}

    def xpeer(k):
        return {"exp": e, "feat": zh * 4 + (x + k) % 4}

    load_enc = pltpu.make_async_copy(enc_hbm, enc_w, load_sem.at[0])
    load_gate = pltpu.make_async_copy(gate_hbm.at[0], gate_w, load_sem.at[1])
    load_up = pltpu.make_async_copy(up_hbm.at[0], up_w, load_sem.at[2])
    load_dec = pltpu.make_async_copy(dec_hbm, dec_w.at[:, pl.ds(0, WIDTH)], load_sem.at[3])
    load_down = pltpu.make_async_copy(down_hbm.at[0], down_w, load_sem.at[4])
    small = [
        pltpu.make_async_copy(source, target, load_sem.at[5 + n])
        for n, (source, target) in enumerate(
            (
                (route_hbm, route_ref),
                (weight_hbm, weight_ref),
                (tok_hbm, tok_all.at[e, :, pl.ds(0, WIDTH)]),
                (ids_hbm, ids_ref),
                (values_hbm, values_ref),
                (bias_hbm, bias_ref),
            )
        )
    ]
    for load in small:
        load.start()
    for load in (load_enc, load_gate, load_up, load_dec, load_down):
        load.start()

    barrier = pltpu.get_barrier_semaphore()

    def greet(k, carry):
        pl.semaphore_signal(
            barrier, inc=1, device_id={"exp": (e + k) % EXPERTS, "feat": f}, device_id_type=MESH
        )
        return carry

    lax.fori_loop(1, EXPERTS, greet, 0)
    for k in (1, 3):
        pl.semaphore_signal(barrier, inc=1, device_id=xpeer(k), device_id_type=MESH)
    pl.semaphore_signal(barrier, inc=1, device_id=zpeer, device_id_type=MESH)
    small[0].wait()
    small[1].wait()
    expert_of = lax.broadcasted_iota(jnp.int32, (EXTRA, ROWS), 0)
    named = jnp.zeros((EXTRA, ROWS), F32)
    spread = jnp.zeros((EXTRA, ROWS), F32)
    for k in range(route_ref.shape[0]):
        hit = route_ref[k : k + 1, :] == expert_of
        named = jnp.where(hit, 1.0, named)
        spread = jnp.where(hit, weight_ref[k : k + 1, :], spread)
    one = lax.broadcasted_iota(jnp.int32, (ROWS, ROWS), 0)
    other = lax.broadcasted_iota(jnp.int32, (ROWS, ROWS), 1)
    before = dot(named.astype(BF16), jnp.where(one < other, 1.0, 0.0).astype(BF16))
    code_t = jnp.where((named > 0) & (before < SLOT), before + 1.0, 0.0).astype(BF16)
    code = lax.dot_general(
        jnp.where(one == other, 1.0, 0.0).astype(BF16),
        code_t,
        (((1,), (1,)), ((), ())),
        preferred_element_type=F32,
    ).astype(BF16)
    small[2].wait()
    tok_all[e, :, pl.ds(WIDTH, EXTRA)] = code
    pl.semaphore_wait(barrier, EXPERTS - 1 + 3)

    def same_core(there_y, there_z):
        return {"exp": (there_y * 4 + there_z) * 2 + core, "feat": f}

    def block_at(back_y, back_z, which):
        return (((y + 4 - back_y) % 4) * 4 + (zl + 4 - back_z) % 4) * 2 + which

    def token_z(k):
        return remote(
            tok_all.at[e], tok_all.at[e], sent.at[0], tz_r.at[k - 1], same_core(y, (zl + k) % 4)
        )

    def token_z_arrival(k):
        block = block_at(0, k, core)
        return remote(tok_all.at[block], tok_all.at[block], sent.at[0], tz_r.at[k - 1], mate)

    def token_y(k, m):
        block = block_at(0, m, core)
        at = (k - 1) * 4 + m
        return remote(
            tok_all.at[block], tok_all.at[block], sent.at[0], ty_r.at[at], same_core((y + k) % 4, zl)
        )

    def token_y_arrival(k, m):
        block = block_at(k, m, core)
        at = (k - 1) * 4 + m
        return remote(tok_all.at[block], tok_all.at[block], sent.at[0], ty_r.at[at], mate)

    def token_pass(k, m):
        block = block_at(k, m, core)
        return remote(tok_all.at[block], tok_all.at[block], sent.at[0], mate_r.at[k], mate)

    def four_passed(k):
        four = tok_all.at[pl.ds(0, 4)]
        return remote(four, four, sent.at[0], mate_r.at[k], mate)

    for k in (1, 3, 2):
        token_z(k).start()
    token_pass(0, 0).start()
    for k in (2, 1, 3):
        token_y(k, 0).start()
    for m in (1, 3, 2):
        token_z_arrival(m).wait_recv()
        token_pass(0, m).start()
        for k in (2, 1, 3):
            token_y(k, m).start()

    def from_y(k):
        for m in (0, 1, 3, 2):
            token_y_arrival(k, m).wait_recv()
            token_pass(k, m).start()

    def from_mate(k):
        four_passed(k).wait_recv()

    clamps = ids_ref.shape[1]

    def three(value):
        high = value.astype(BF16)
        rest = value - high.astype(F32)
        middle = rest.astype(BF16)
        return high, middle, (rest - middle.astype(F32)).astype(BF16)

    def route_weights():
        slot_lane = lax.broadcasted_iota(jnp.int32, (EXTRA, EXPERTS * SLOT), 1)
        widen = jnp.where(
            (slot_lane >> 3) == lax.broadcasted_iota(jnp.int32, (EXTRA, EXPERTS * SLOT), 0), 1.0, 0.0
        ).astype(BF16)
        slot_wanted = (
            (lax.broadcasted_iota(jnp.int32, (ROWS, EXPERTS * SLOT), 1) & 7) + 1
        ).astype(F32)
        in_slot = dot(code, widen) == slot_wanted

        for part, piece in enumerate(three(spread)):
            widened = lax.dot_general(
                piece, widen, (((0,), (0,)), ((), ())), preferred_element_type=F32
            )
            combine[part] = jnp.where(in_slot, widened, 0.0).astype(BF16)

    def listed_columns():
        small[3].wait()
        feature = lax.broadcasted_iota(jnp.int32, (FEATURES, clamps), 0) + e * FEATURES
        listed_col = jnp.where(feature == ids_ref[...], 1.0, 0.0).astype(BF16)
        dec_w[:, pl.ds(WIDTH, EXTRA)] = jnp.concatenate(
            [listed_col, jnp.zeros((FEATURES, EXTRA - clamps), BF16)], axis=1
        )

    toward = (1, 3)

    def quarter(k):
        return (x + k) % 4

    def half_rows(k, half, size):
        return pl.ds(pl.multiple_of(quarter(k) * 2 * size + half * size, size), size)

    def gu_rows(h, k, half):
        return pl.ds(pl.multiple_of(h * 128 + quarter(k) * 32 + half * 16, 16), 16)

    def gu_ring_copy(h, n):
        return remote(
            gu_own.at[gu_rows(h, 2, n)],
            gu_ring.at[h, n],
            sent.at[1],
            gux_r.at[h, n],
            xpeer(toward[n]),
        )

    def gu_early(h, n):
        return remote(
            gu_own.at[gu_rows(h, toward[n], 1 - n)],
            gu_in.at[h, 1 - n, 0],
            sent.at[1],
            gux_r.at[h, 2],
            xpeer(toward[n]),
        )

    def gu_late(h, n):
        return remote(
            gu_own.at[gu_rows(h, toward[n], n)],
            gu_in.at[h, n, 1],
            sent.at[1],
            gux_r.at[h, 2],
            xpeer(toward[n]),
        )

    def gu_relay(h):
        for n in (0, 1):
            gu_ring_copy(h, n).wait_recv()
            rows = gu_rows(h, toward[n], n)
            gu_own[rows, :] = gu_own[rows, :] + gu_ring[h, n]
            gu_late(h, n).start()

    def gu_pick():
        everything = tok_all[...].reshape(EXPERTS * ROWS, WIDE)
        pick = jnp.where(lax.broadcasted_iota(jnp.int32, (8, EXTRA), 1) == e, 1.0, 0.0).astype(BF16)
        codes = lax.dot_general(
            pick, everything[:, WIDTH:], (((1,), (1,)), ((), ())), preferred_element_type=F32
        )
        slot_row = lax.broadcasted_iota(jnp.int32, (EXPERTS * SLOT, EXPERTS * ROWS), 0)
        token_col = lax.broadcasted_iota(jnp.int32, (EXPERTS * SLOT, EXPERTS * ROWS), 1)
        same_block = (((slot_row >> 3) + e) & (EXPERTS - 1)) == (token_col >> 4)
        wanted = ((slot_row & 7) + 1).astype(F32)
        picker = jnp.where(same_block & (codes[0:1, :] == wanted), 1.0, 0.0).astype(BF16)
        expert_in[...] = dot(picker, everything[:, :WIDTH]).astype(BF16)
        load_gate.wait()
        load_up.wait()

    def gu_multiply(h):
        rows = pl.ds(h * 128, 128)
        for half, weights in ((0, gate_w), (1, up_w)):

            def gate_tile(n, carry, half=half, weights=weights):
                at = pl.multiple_of(n * 256, 256)
                gu_own[rows, pl.ds(pl.multiple_of(half * HIDDEN + n * 256, 256), 256)] = dot(
                    expert_in[rows, :], weights[:, pl.ds(at, 256)]
                )
                return carry

            lax.fori_loop(0, HIDDEN // 256, gate_tile, 0)
        for n in (0, 1):
            gu_ring_copy(h, n).start()
        for n in (0, 1):
            gu_early(h, n).start()

    def blocks_of(j):
        return ((y + j) % 4) * 8

    def pre_ring_copy(j, n):
        return remote(
            pre_send.at[j, half_rows(2, n, 16)],
            pre_ring.at[j, n],
            sent.at[2],
            px_r.at[j, n],
            xpeer(toward[n]),
        )

    def pre_early(j, n):
        return remote(
            pre_send.at[j, half_rows(toward[n], 1 - n, 16)],
            pre_in.at[j, 1 - n, 0],
            sent.at[2],
            px_r.at[j, 2],
            xpeer(toward[n]),
        )

    def pre_late(j, n):
        return remote(
            pre_send.at[j, half_rows(toward[n], n, 16)],
            pre_in.at[j, n, 1],
            sent.at[2],
            px_r.at[j, 2],
            xpeer(toward[n]),
        )

    def pre_relay(j):
        for n in (0, 1):
            pre_ring_copy(j, n).wait_recv()
            rows = half_rows(toward[n], n, 16)
            pre_send[j, rows, :] = (pre_f32[j, rows, :] + pre_ring[j, n].astype(F32)).astype(BF16)
            pre_late(j, n).start()

    def pre_multiply(j):
        rows = tok_all[pl.ds(blocks_of(j), 8)].reshape(CHUNK_ROWS, WIDE)[:, :WIDTH]

        def tile(n, carry):
            at = pl.multiple_of(n * 256, 256)
            part = dot(rows, enc_w[:, pl.ds(at, 256)])
            pre_f32[j, :, pl.ds(at, 256)] = part
            pre_send[j, :, pl.ds(at, 256)] = part.astype(BF16)
            return carry

        lax.fori_loop(0, FEATURES // 256, tile, 0)
        for n in (0, 1):
            pre_ring_copy(j, n).start()
        for n in (0, 1):
            pre_early(j, n).start()

    def pz_copy(j):
        return remote(z_send.at[j], z_in.at[j], sent.at[2], pz_r.at[j], zpeer)

    def pre_reduce(j):
        remote(pre_in.at[j], pre_in.at[j], sent.at[2], px_r.at[j, 2], mate).wait_recv()
        for half in (0, 1):
            total = pre_f32[j, half_rows(0, half, 16), :]
            for k in range(2):
                total = total + pre_in[j, half, k].astype(F32)
            z_own[j, half] = total
            z_send[j, half] = total.astype(BF16)
        pz_copy(j).start()

    def block_of(j, k, side):
        return blocks_of(j) + 2 * quarter(k) + side

    def ax_copy(j, n, side):
        block = block_of(j, 0, side)
        at = n if n == side else 2
        return remote(act.at[block], act.at[block], sent.at[3], ax_r.at[j, at], xpeer(toward[n]))

    def ax_relay(j, n):
        block = block_of(j, toward[1 - n], n)
        return remote(act.at[block], act.at[block], sent.at[3], ax_r.at[j, 2], xpeer(toward[n]))

    def activate(j):
        pz_copy(j).wait_recv()
        for side in (0, 1):
            pre = z_own[j, side] + z_in[j, side].astype(F32) + bias_ref[...]
            act[block_of(j, 0, side)] = jnp.maximum(pre, 0.0).astype(BF16)
        for side in (0, 1):
            for n in (0, 1):
                ax_copy(j, n, n if side == 0 else 1 - n).start()

    def relay(j):
        ax_copy(j, 0, 0).wait_recv()
        ax_relay(j, 0).start()
        ax_copy(j, 1, 1).wait_recv()
        ax_relay(j, 1).start()

    def guz_copy(h):
        return remote(gu_zsend.at[h], gu_zin.at[h], sent.at[1], guz_r.at[h], zpeer)

    def gu_reduce(h):
        remote(gu_in.at[h], gu_in.at[h], sent.at[1], gux_r.at[h, 2], mate).wait_recv()
        for keep in (0, 1):
            half = 1 - zh if keep == 0 else zh
            mine = gu_rows(h, 0, half)
            total = gu_own[mine, :] + gu_in[h, half, 0] + gu_in[h, half, 1]
            if keep == 0:
                gu_zsend[h] = total.astype(BF16)
                guz_copy(h).start()
            else:
                gu_own[mine, :] = total

    def hid_of(h, k, side):
        return h * 8 + 2 * quarter(k) + side

    def hz_copy(h):
        part = hid_of(h, 0, zh)
        return remote(hid.at[part], hid.at[part], sent.at[4], hz_r.at[h], zpeer)

    def hx_copy(h, n, second):
        part = hid_of(h, 0, (1 - zh) if second else zh)
        at = n if n == second else 2
        return remote(hid.at[part], hid.at[part], sent.at[4], hx_r.at[h, at], xpeer(toward[n]))

    def hx_relay(h, n):
        part = hid_of(h, toward[1 - n], zh if n == 0 else 1 - zh)
        return remote(hid.at[part], hid.at[part], sent.at[4], hx_r.at[h, 2], xpeer(toward[n]))

    def gu_activate(h):
        guz_copy(h).wait_recv()
        total = gu_own[gu_rows(h, 0, zh), :] + gu_zin[h].astype(F32)
        gate, up = total[:, :HIDDEN], total[:, HIDDEN:]
        hid[hid_of(h, 0, zh)] = (gate / (1.0 + jnp.exp(-gate)) * up).astype(BF16)
        hz_copy(h).start()
        for n in (0, 1):
            hx_copy(h, n, 0).start()

    def gu_pass_on(h):
        hz_copy(h).wait_recv()
        for n in (1, 0):
            hx_copy(h, n, 1).start()

    def hid_relay(h):
        hx_copy(h, 0, 0).wait_recv()
        hx_relay(h, 0).start()
        hx_copy(h, 1, 1).wait_recv()
        hx_relay(h, 1).start()

    def out_copy(k):
        there = (e + k) % EXPERTS
        return remote(
            out_send.at[k], out_in.at[e], sent.at[5], out_r.at[0], {"exp": there, "feat": f}
        )

    def down(h):
        four = hid.at[pl.ds(0, 4)]
        remote(four, four, sent.at[4], hx_r.at[h, 2], mate).wait_recv()
        hidden = hid[pl.ds(h * 8, 8)].reshape(128, HIDDEN)
        for n in range(7):
            cols = pl.ds(n * 128, 128)
            out_send[pl.ds(h * 16, 16), :, cols] = (
                dot(hidden, down_w[:, cols]).reshape(16, SLOT, 128).astype(BF16)
            )
        if h == 0:
            out_in[e] = out_send[0]

        def start(k, carry):
            out_copy(k).start()
            return carry

        lax.fori_loop(1 if h == 0 else 16, h * 16 + 16, start, 0)

    def cm_copy(j):
        return remote(rec.at[j, 1 - core], mate_in.at[j], sent.at[6], cm_r.at[j], mate)

    def decode(j):
        four = act.at[pl.ds(0, 4)]
        remote(four, four, sent.at[3], ax_r.at[j, 2], mate).wait_recv()
        rows = act[pl.ds(blocks_of(j), 8)].reshape(CHUNK_ROWS, FEATURES)

        def tile(n, carry):
            at = pl.multiple_of(n * 256, 256)
            part = dot(rows, dec_w[:, pl.ds(at, 256)]).reshape(4, 2, ROWS, 256)
            for c in (0, 1):
                rec[j, c, :, :, pl.ds(at, 256)] = part[:, c]
            return carry

        lax.fori_loop(0, WIDE // 256, tile, 0)
        cm_copy(j).start()

    def fin_copy(j):
        return remote(
            fin_send.at[j], fin_in.at[j], sent.at[7], fin_r.at[0], same_core((y + j) % 4, zl)
        )

    def fin_z_copy(k):
        return remote(
            fin_zsend.at[k], fin_zin.at[k], sent.at[7], fin_r.at[1], same_core(y, (zl + k) % 4)
        )

    def finish(j):
        cm_copy(j).wait_recv()
        for to in range(4):
            total = rec[j, core, to] + mate_in[j, to]
            if j == 0:
                fin_own[to] = total
            else:
                fin_send[j, to] = total.astype(BF16)
        if j > 0:
            fin_copy(j).start()

    def finish_z():
        most = fin_in.at[pl.ds(1, 3)]
        remote(most, most, sent.at[7], fin_r.at[0], mate).wait_recv()
        for k in (1, 3, 2, 0):
            to = (zl + k) % 4
            total = fin_own[to]
            for j in range(1, CHUNKS):
                total = total + fin_in[j, to].astype(F32)
            if k == 0:
                fin_zin[0] = total
            else:
                fin_zsend[k] = total
                fin_z_copy(k).start()

    def row_mate_copy():
        return remote(row_own, row_mate, sent.at[8], rm_r.at[0], mate)

    def row_y_copy(k):
        there = (y + k) % 4
        return remote(
            row_part.at[there], row_in.at[k - 1], sent.at[8], ry_r.at[k - 1], same_core(there, zl)
        )

    def row_z_copy(k):
        return remote(
            row_sum, row_zin.at[k - 1], sent.at[8], rz_r.at[k - 1], same_core(y, (zl + k) % 4)
        )

    def row_gather_copy(k):
        return remote(
            rows_dec.at[y], rows_dec.at[y], sent.at[8], rg_r.at[k - 1], same_core((y + k) % 4, zl)
        )

    def rows_start():
        mine = lax.dot_general(
            dec_w[:, pl.ds(WIDTH, EXTRA)],
            dec_w[:, pl.ds(0, WIDTH)],
            (((0,), (0,)), ((), ())),
            preferred_element_type=F32,
        )
        row_own[...] = mine[:64].astype(BF16).reshape(4, ROWS, WIDTH)
        row_mate_copy().start()

    def rows_y():
        row_mate_copy().wait_recv()
        row_part[...] = (row_own[...].astype(F32) + row_mate[...].astype(F32)).astype(BF16)
        for k in range(1, 4):
            row_y_copy(k).start()

    def rows_z():
        total = row_part[y].astype(F32)
        for k in range(1, 4):
            row_y_copy(k).wait_recv()
            total = total + row_in[k - 1].astype(F32)
        row_sum[...] = total.astype(BF16)
        for k in range(1, 4):
            row_z_copy(k).start()

    def rows_gather():
        total = row_sum[...].astype(F32)
        for k in range(1, 4):
            row_z_copy(k).wait_recv()
            total = total + row_zin[k - 1].astype(F32)
        rows_dec[y] = total.astype(BF16)
        for k in range(1, 4):
            row_gather_copy(k).start()

    def combine_moe():
        most = out_in.at[pl.ds(1, EXPERTS - 1)]
        remote(most, most, sent.at[5], out_r.at[0], mate).wait_recv()
        for n in range(7):
            cols = pl.ds(n * 128, 128)
            rows = out_in[:, :, cols].astype(F32).reshape(EXPERTS * SLOT, 128).astype(BF16)
            moe_ref[:, cols] = dot(combine[2], rows) + dot(combine[1], rows) + dot(combine[0], rows)
        write_moe.start()

    def total_up():
        most = fin_zin.at[pl.ds(1, 3)]
        remote(most, most, sent.at[7], fin_r.at[1], mate).wait_recv()
        total = (fin_zin[0] + fin_zin[1]) + (fin_zin[2] + fin_zin[3])
        recon_ref[...] = total[:, :WIDTH]
        write_recon.start()
        for k in range(1, 4):
            row_gather_copy(k).wait_recv()
        small[4].wait()
        change = values_ref[...].astype(F32) - total[:, WIDTH : WIDTH + clamps]
        listed = rows_dec[...].reshape(64, WIDTH)
        high, middle, low = three(change)
        shift_ref[...] = dot(low, listed) + dot(middle, listed) + dot(high, listed)
        write_shift.start()

    write_recon = pltpu.make_async_copy(recon_ref, recon_hbm, load_sem.at[11])
    write_moe = pltpu.make_async_copy(moe_ref, moe_hbm, load_sem.at[12])
    write_shift = pltpu.make_async_copy(shift_ref, shift_hbm, load_sem.at[13])

    from_mate(0)
    load_enc.wait()
    pre_multiply(0)
    for k in (1, 3, 2):
        from_y(k)
    for k in (1, 3, 2):
        from_mate(k)
    gu_pick()
    pre_relay(0)
    pre_multiply(2)
    gu_multiply(1)
    pre_multiply(3)
    pre_relay(2)
    gu_multiply(0)
    pre_reduce(0)
    load_dec.wait()
    listed_columns()
    rows_start()
    gu_relay(1)
    pre_multiply(1)
    pre_relay(3)
    rows_y()
    route_weights()
    pre_reduce(2)
    rows_z()
    gu_relay(0)
    small[5].wait()
    activate(0)
    gu_reduce(1)
    pre_relay(1)
    activate(2)
    rows_gather()
    pre_reduce(3)
    gu_reduce(0)
    gu_activate(1)
    relay(0)
    pre_reduce(1)
    relay(2)
    activate(3)
    decode(0)
    decode(2)
    finish(0)
    relay(3)
    gu_pass_on(1)
    gu_activate(0)
    finish(2)
    activate(1)
    decode(3)
    hid_relay(1)
    gu_pass_on(0)
    relay(1)
    finish(3)
    load_down.wait()
    down(1)
    hid_relay(0)
    decode(1)
    down(0)
    finish(1)
    finish_z()
    combine_moe()
    total_up()

    for kind, ref in (
        (0, tok_all.at[pl.ds(0, 31)]),
        (1, gu_own.at[pl.ds(0, 208)]),
        (2, act),
        (3, act.at[pl.ds(0, 24)]),
        (4, hid.at[pl.ds(0, 14)]),
        (5, out_send.at[pl.ds(1, 31)]),
        (6, mate_in),
        (7, tok_all.at[pl.ds(0, 18)]),
        (8, out_send.at[pl.ds(0, 26)]),
    ):
        remote(ref, ref, sent.at[kind], rm_r.at[0], mate).wait_send()
    for write in (write_recon, write_moe, write_shift):
        write.wait()


def fused(*operands):
    hbm = pl.BlockSpec(memory_space=pl.ANY)
    dma = pltpu.SemaphoreType.DMA
    scratch = [
        pltpu.VMEM((8, ROWS), jnp.int32),
        pltpu.VMEM((8, ROWS), F32),
        pltpu.VMEM((1, FEATURES), F32),
        pltpu.VMEM(operands[4].shape, jnp.int32),
        pltpu.VMEM(operands[5].shape, BF16),
        pltpu.VMEM((ROWS, WIDTH), F32),
        pltpu.VMEM((ROWS, WIDTH), F32),
        pltpu.VMEM((ROWS, WIDTH), F32),
        pltpu.VMEM((EXPERTS * SLOT, WIDTH), BF16),
        pltpu.VMEM((WIDTH, HIDDEN), BF16),
        pltpu.VMEM((WIDTH, HIDDEN), BF16),
        pltpu.VMEM((HIDDEN, WIDTH), BF16),
        pltpu.VMEM((WIDTH, FEATURES), BF16),
        pltpu.VMEM((FEATURES, WIDE), BF16),
        pltpu.VMEM((EXPERTS, ROWS, WIDE), BF16),
        pltpu.VMEM((EXPERTS * SLOT, 2 * HIDDEN), F32),
        pltpu.VMEM((2, 2, ROWS, 2 * HIDDEN), F32),
        pltpu.VMEM((2, 2, 2, ROWS, 2 * HIDDEN), F32),
        pltpu.VMEM((2, ROWS, 2 * HIDDEN), BF16),
        pltpu.VMEM((2, ROWS, 2 * HIDDEN), BF16),
        pltpu.VMEM((CHUNKS, CHUNK_ROWS, FEATURES), F32),
        pltpu.VMEM((CHUNKS, CHUNK_ROWS, FEATURES), BF16),
        pltpu.VMEM((CHUNKS, 2, ROWS, FEATURES), BF16),
        pltpu.VMEM((CHUNKS, 2, 2, ROWS, FEATURES), BF16),
        pltpu.VMEM((CHUNKS, 2, ROWS, FEATURES), BF16),
        pltpu.VMEM((CHUNKS, 2, ROWS, FEATURES), BF16),
        pltpu.VMEM((CHUNKS, 2, ROWS, FEATURES), F32),
        pltpu.VMEM((EXPERTS, ROWS, FEATURES), BF16),
        pltpu.VMEM((2 * 8, ROWS, HIDDEN), BF16),
        pltpu.VMEM((EXPERTS, SLOT, WIDTH), BF16),
        pltpu.VMEM((EXPERTS, SLOT, WIDTH), BF16),
        pltpu.VMEM((CHUNKS, 2, 4, ROWS, WIDE), F32),
        pltpu.VMEM((CHUNKS, 4, ROWS, WIDE), F32),
        pltpu.VMEM((CHUNKS, 4, ROWS, WIDE), BF16),
        pltpu.VMEM((CHUNKS, 4, ROWS, WIDE), BF16),
        pltpu.VMEM((4, ROWS, WIDE), F32),
        pltpu.VMEM((4, ROWS, WIDE), F32),
        pltpu.VMEM((4, ROWS, WIDE), F32),
        pltpu.VMEM((3, ROWS, EXPERTS * SLOT), BF16),
        pltpu.VMEM((4, ROWS, WIDTH), BF16),
        pltpu.VMEM((4, ROWS, WIDTH), BF16),
        pltpu.VMEM((4, ROWS, WIDTH), BF16),
        pltpu.VMEM((3, ROWS, WIDTH), BF16),
        pltpu.VMEM((ROWS, WIDTH), BF16),
        pltpu.VMEM((3, ROWS, WIDTH), BF16),
        pltpu.VMEM((4, ROWS, WIDTH), BF16),
        dma((14,)),
        dma((9,)),
        dma((3,)),
        dma((12,)),
        dma((4,)),
        dma((2, 3)),
        dma((2,)),
        dma((2,)),
        dma((2, 3)),
        dma((CHUNKS, 3)),
        dma((CHUNKS,)),
        dma((CHUNKS, 3)),
        dma((1,)),
        dma((CHUNKS,)),
        dma((2,)),
        dma((1,)),
        dma((3,)),
        dma((3,)),
        dma((3,)),
    ]
    return pl.pallas_call(
        kernel,
        out_shape=(
            jax.ShapeDtypeStruct((ROWS, WIDTH), F32),
            jax.ShapeDtypeStruct((ROWS, WIDTH), F32),
            jax.ShapeDtypeStruct((ROWS, WIDTH), F32),
        ),
        in_specs=[hbm] * 11,
        out_specs=(hbm, hbm, hbm),
        scratch_shapes=scratch,
        name="fused_layer",
        cost_estimate=pl.CostEstimate(
            flops=6_000_000_000, bytes_accessed=400_000_000, transcendentals=0
        ),
        compiler_params=pltpu.CompilerParams(
            collective_id=0, has_side_effects=True, vmem_limit_bytes=56 << 20
        ),
    )(*operands)


def local(
    tokens,
    route_ids,
    route_weights,
    gate_proj,
    up_proj,
    down_proj,
    enc_weight,
    enc_bias,
    dec_weight,
    dec_bias,
    clamp_ids,
    clamp_values,
):
    recon, moe_out, shift = fused(
        tokens,
        route_ids.T,
        route_weights.T,
        enc_bias[None, :],
        clamp_ids[None, :],
        clamp_values[None, :],
        gate_proj,
        up_proj,
        down_proj,
        enc_weight,
        dec_weight,
    )
    return moe_out - recon - dec_bias, moe_out + shift


def solution(mesh):
    placed = (
        P("exp", "feat"),
        P("exp", None),
        P("exp", None),
        P("exp", "feat", None),
        P("exp", "feat", None),
        P("exp", None, "feat"),
        P("feat", "exp"),
        P("exp"),
        P("exp", "feat"),
        P("feat"),
        P(),
        P(),
    )
    return jax.shard_map(
        local,
        mesh=mesh,
        in_specs=placed,
        out_specs=(P("exp", "feat"), P("exp", "feat")),
        check_vma=False,
    )
```

```python
import functools

import jax
import jax.numpy as jnp
from jax import lax
from jax.experimental import pallas as pl
from jax.experimental.pallas import tpu as pltpu
from jax.sharding import PartitionSpec as P

SLOT = 8
ROWS = 16
WIDTH = 896
EXTRA = 128
WIDE = WIDTH + EXTRA
FEATURES = 2048
HIDDEN = 1024
CHIPS = 16
EXPERTS = 32
CHUNKS = 4
CHUNK_ROWS = 128
MESH = pl.DeviceIdType.MESH
F32 = jnp.float32
BF16 = jnp.bfloat16


def remote(src, dst, send_sem, recv_sem, device):
    return pltpu.make_async_remote_copy(
        src_ref=src,
        dst_ref=dst,
        send_sem=send_sem,
        recv_sem=recv_sem,
        device_id=device,
        device_id_type=MESH,
    )


def dot(a, b):
    return jnp.dot(a, b, preferred_element_type=F32)


def kernel(
    tok_hbm,
    route_hbm,
    weight_hbm,
    bias_hbm,
    ids_hbm,
    values_hbm,
    gate_hbm,
    up_hbm,
    down_hbm,
    enc_hbm,
    dec_hbm,
    recon_hbm,
    moe_hbm,
    shift_hbm,
    route_ref,
    weight_ref,
    bias_ref,
    ids_ref,
    values_ref,
    recon_ref,
    moe_ref,
    shift_ref,
    expert_in,
    gate_w,
    up_w,
    down_w,
    enc_w,
    dec_w,
    tok_all,
    gu_own,
    gu_ring,
    gu_in,
    gu_zsend,
    gu_zin,
    pre_f32,
    pre_send,
    pre_ring,
    pre_in,
    z_send,
    z_in,
    z_own,
    act,
    hid,
    out_send,
    out_in,
    rec,
    mate_in,
    fin_send,
    fin_in,
    fin_own,
    fin_zsend,
    fin_zin,
    combine,
    row_own,
    row_mate,
    row_part,
    row_in,
    row_sum,
    row_zin,
    rows_dec,
    load_sem,
    sent,
    tz_r,
    ty_r,
    mate_r,
    gux_r,
    guz_r,
    hz_r,
    hx_r,
    px_r,
    pz_r,
    ax_r,
    out_r,
    cm_r,
    fin_r,
    rm_r,
    ry_r,
    rz_r,
    rg_r,
):
    e = lax.axis_index("exp")
    f = lax.axis_index("feat")
    chip, core = e // 2, e % 2
    y, zl = chip // 4, chip % 4
    zh, x = f // 4, f % 4
    mate = {"exp": chip * 2 + (1 - core), "feat": f}
    zpeer = {"exp": e, "feat": (1 - zh) * 4 + x}

    def xpeer(k):
        return {"exp": e, "feat": zh * 4 + (x + k) % 4}

    load_enc = pltpu.make_async_copy(enc_hbm, enc_w, load_sem.at[0])
    load_gate = pltpu.make_async_copy(gate_hbm.at[0], gate_w, load_sem.at[1])
    load_up = pltpu.make_async_copy(up_hbm.at[0], up_w, load_sem.at[2])
    load_dec = pltpu.make_async_copy(dec_hbm, dec_w.at[:, pl.ds(0, WIDTH)], load_sem.at[3])
    load_down = pltpu.make_async_copy(down_hbm.at[0], down_w, load_sem.at[4])
    small = [
        pltpu.make_async_copy(source, target, load_sem.at[5 + n])
        for n, (source, target) in enumerate(
            (
                (route_hbm, route_ref),
                (weight_hbm, weight_ref),
                (tok_hbm, tok_all.at[e, :, pl.ds(0, WIDTH)]),
                (ids_hbm, ids_ref),
                (values_hbm, values_ref),
                (bias_hbm, bias_ref),
            )
        )
    ]
    for load in small:
        load.start()
    for load in (load_enc, load_gate, load_up, load_dec, load_down):
        load.start()

    barrier = pltpu.get_barrier_semaphore()

    def greet(k, carry):
        pl.semaphore_signal(
            barrier, inc=1, device_id={"exp": (e + k) % EXPERTS, "feat": f}, device_id_type=MESH
        )
        return carry

    lax.fori_loop(1, EXPERTS, greet, 0)
    for k in (1, 3):
        pl.semaphore_signal(barrier, inc=1, device_id=xpeer(k), device_id_type=MESH)
    pl.semaphore_signal(barrier, inc=1, device_id=zpeer, device_id_type=MESH)
    small[0].wait()
    small[1].wait()
    expert_of = lax.broadcasted_iota(jnp.int32, (EXTRA, ROWS), 0)
    named = jnp.zeros((EXTRA, ROWS), F32)
    spread = jnp.zeros((EXTRA, ROWS), F32)
    for k in range(route_ref.shape[0]):
        hit = route_ref[k : k + 1, :] == expert_of
        named = jnp.where(hit, 1.0, named)
        spread = jnp.where(hit, weight_ref[k : k + 1, :], spread)
    one = lax.broadcasted_iota(jnp.int32, (ROWS, ROWS), 0)
    other = lax.broadcasted_iota(jnp.int32, (ROWS, ROWS), 1)
    before = dot(named.astype(BF16), jnp.where(one < other, 1.0, 0.0).astype(BF16))
    code_t = jnp.where((named > 0) & (before < SLOT), before + 1.0, 0.0).astype(BF16)
    code = lax.dot_general(
        jnp.where(one == other, 1.0, 0.0).astype(BF16),
        code_t,
        (((1,), (1,)), ((), ())),
        preferred_element_type=F32,
    ).astype(BF16)
    small[2].wait()
    tok_all[e, :, pl.ds(WIDTH, EXTRA)] = code
    pl.semaphore_wait(barrier, EXPERTS - 1 + 3)

    def same_core(there_y, there_z):
        return {"exp": (there_y * 4 + there_z) * 2 + core, "feat": f}

    def block_at(back_y, back_z, which):
        return (((y + 4 - back_y) % 4) * 4 + (zl + 4 - back_z) % 4) * 2 + which

    def token_z(k):
        return remote(
            tok_all.at[e], tok_all.at[e], sent.at[0], tz_r.at[k - 1], same_core(y, (zl + k) % 4)
        )

    def token_z_arrival(k):
        block = block_at(0, k, core)
        return remote(tok_all.at[block], tok_all.at[block], sent.at[0], tz_r.at[k - 1], mate)

    def token_y(k, m):
        block = block_at(0, m, core)
        at = (k - 1) * 4 + m
        return remote(
            tok_all.at[block], tok_all.at[block], sent.at[0], ty_r.at[at], same_core((y + k) % 4, zl)
        )

    def token_y_arrival(k, m):
        block = block_at(k, m, core)
        at = (k - 1) * 4 + m
        return remote(tok_all.at[block], tok_all.at[block], sent.at[0], ty_r.at[at], mate)

    def token_pass(k, m):
        block = block_at(k, m, core)
        return remote(tok_all.at[block], tok_all.at[block], sent.at[0], mate_r.at[k], mate)

    def four_passed(k):
        four = tok_all.at[pl.ds(0, 4)]
        return remote(four, four, sent.at[0], mate_r.at[k], mate)

    for k in (1, 3, 2):
        token_z(k).start()
    token_pass(0, 0).start()
    for k in (2, 1, 3):
        token_y(k, 0).start()
    for m in (1, 3, 2):
        token_z_arrival(m).wait_recv()
        token_pass(0, m).start()
        for k in (2, 1, 3):
            token_y(k, m).start()

    def from_y(k):
        for m in (0, 1, 3, 2):
            token_y_arrival(k, m).wait_recv()
            token_pass(k, m).start()

    def from_mate(k):
        four_passed(k).wait_recv()

    clamps = ids_ref.shape[1]

    def three(value):
        high = value.astype(BF16)
        rest = value - high.astype(F32)
        middle = rest.astype(BF16)
        return high, middle, (rest - middle.astype(F32)).astype(BF16)

    def route_weights():
        slot_lane = lax.broadcasted_iota(jnp.int32, (EXTRA, EXPERTS * SLOT), 1)
        widen = jnp.where(
            (slot_lane >> 3) == lax.broadcasted_iota(jnp.int32, (EXTRA, EXPERTS * SLOT), 0), 1.0, 0.0
        ).astype(BF16)
        slot_wanted = (
            (lax.broadcasted_iota(jnp.int32, (ROWS, EXPERTS * SLOT), 1) & 7) + 1
        ).astype(F32)
        in_slot = dot(code, widen) == slot_wanted

        for part, piece in enumerate(three(spread)):
            widened = lax.dot_general(
                piece, widen, (((0,), (0,)), ((), ())), preferred_element_type=F32
            )
            combine[part] = jnp.where(in_slot, widened, 0.0).astype(BF16)

    def listed_columns():
        small[3].wait()
        feature = lax.broadcasted_iota(jnp.int32, (FEATURES, clamps), 0) + e * FEATURES
        listed_col = jnp.where(feature == ids_ref[...], 1.0, 0.0).astype(BF16)
        dec_w[:, pl.ds(WIDTH, EXTRA)] = jnp.concatenate(
            [listed_col, jnp.zeros((FEATURES, EXTRA - clamps), BF16)], axis=1
        )

    toward = (1, 3)

    def quarter(k):
        return (x + k) % 4

    def half_rows(k, half, size):
        return pl.ds(pl.multiple_of(quarter(k) * 2 * size + half * size, size), size)

    def gu_rows(h, k, half):
        return pl.ds(pl.multiple_of(h * 128 + quarter(k) * 32 + half * 16, 16), 16)

    def gu_ring_copy(h, n):
        return remote(
            gu_own.at[gu_rows(h, 2, n)],
            gu_ring.at[h, n],
            sent.at[1],
            gux_r.at[h, n],
            xpeer(toward[n]),
        )

    def gu_early(h, n):
        return remote(
            gu_own.at[gu_rows(h, toward[n], 1 - n)],
            gu_in.at[h, 1 - n, 0],
            sent.at[1],
            gux_r.at[h, 2],
            xpeer(toward[n]),
        )

    def gu_late(h, n):
        return remote(
            gu_own.at[gu_rows(h, toward[n], n)],
            gu_in.at[h, n, 1],
            sent.at[1],
            gux_r.at[h, 2],
            xpeer(toward[n]),
        )

    def gu_relay(h):
        for n in (0, 1):
            gu_ring_copy(h, n).wait_recv()
            rows = gu_rows(h, toward[n], n)
            gu_own[rows, :] = gu_own[rows, :] + gu_ring[h, n]
            gu_late(h, n).start()

    def gu_pick():
        everything = tok_all[...].reshape(EXPERTS * ROWS, WIDE)
        pick = jnp.where(lax.broadcasted_iota(jnp.int32, (8, EXTRA), 1) == e, 1.0, 0.0).astype(BF16)
        codes = lax.dot_general(
            pick, everything[:, WIDTH:], (((1,), (1,)), ((), ())), preferred_element_type=F32
        )
        slot_row = lax.broadcasted_iota(jnp.int32, (EXPERTS * SLOT, EXPERTS * ROWS), 0)
        token_col = lax.broadcasted_iota(jnp.int32, (EXPERTS * SLOT, EXPERTS * ROWS), 1)
        same_block = (((slot_row >> 3) + e) & (EXPERTS - 1)) == (token_col >> 4)
        wanted = ((slot_row & 7) + 1).astype(F32)
        picker = jnp.where(same_block & (codes[0:1, :] == wanted), 1.0, 0.0).astype(BF16)
        expert_in[...] = dot(picker, everything[:, :WIDTH]).astype(BF16)
        load_gate.wait()
        load_up.wait()

    def gu_multiply(h):
        rows = pl.ds(h * 128, 128)
        for half, weights in ((0, gate_w), (1, up_w)):

            def gate_tile(n, carry, half=half, weights=weights):
                at = pl.multiple_of(n * 256, 256)
                gu_own[rows, pl.ds(pl.multiple_of(half * HIDDEN + n * 256, 256), 256)] = dot(
                    expert_in[rows, :], weights[:, pl.ds(at, 256)]
                )
                return carry

            lax.fori_loop(0, HIDDEN // 256, gate_tile, 0)
        for n in (0, 1):
            gu_ring_copy(h, n).start()
        for n in (0, 1):
            gu_early(h, n).start()

    def blocks_of(j):
        return ((y + j) % 4) * 8

    def pre_ring_copy(j, n):
        return remote(
            pre_send.at[j, half_rows(2, n, 16)],
            pre_ring.at[j, n],
            sent.at[2],
            px_r.at[j, n],
            xpeer(toward[n]),
        )

    def pre_early(j, n):
        return remote(
            pre_send.at[j, half_rows(toward[n], 1 - n, 16)],
            pre_in.at[j, 1 - n, 0],
            sent.at[2],
            px_r.at[j, 2],
            xpeer(toward[n]),
        )

    def pre_late(j, n):
        return remote(
            pre_send.at[j, half_rows(toward[n], n, 16)],
            pre_in.at[j, n, 1],
            sent.at[2],
            px_r.at[j, 2],
            xpeer(toward[n]),
        )

    def pre_relay(j):
        for n in (0, 1):
            pre_ring_copy(j, n).wait_recv()
            rows = half_rows(toward[n], n, 16)
            pre_send[j, rows, :] = (pre_f32[j, rows, :] + pre_ring[j, n].astype(F32)).astype(BF16)
            pre_late(j, n).start()

    def pre_multiply(j):
        rows = tok_all[pl.ds(blocks_of(j), 8)].reshape(CHUNK_ROWS, WIDE)[:, :WIDTH]

        def tile(n, carry):
            at = pl.multiple_of(n * 256, 256)
            part = dot(rows, enc_w[:, pl.ds(at, 256)])
            pre_f32[j, :, pl.ds(at, 256)] = part
            pre_send[j, :, pl.ds(at, 256)] = part.astype(BF16)
            return carry

        lax.fori_loop(0, FEATURES // 256, tile, 0)
        for n in (0, 1):
            pre_ring_copy(j, n).start()
        for n in (0, 1):
            pre_early(j, n).start()

    def pz_copy(j):
        return remote(z_send.at[j], z_in.at[j], sent.at[2], pz_r.at[j], zpeer)

    def pre_reduce(j):
        remote(pre_in.at[j], pre_in.at[j], sent.at[2], px_r.at[j, 2], mate).wait_recv()
        for half in (0, 1):
            total = pre_f32[j, half_rows(0, half, 16), :]
            for k in range(2):
                total = total + pre_in[j, half, k].astype(F32)
            z_own[j, half] = total
            z_send[j, half] = total.astype(BF16)
        pz_copy(j).start()

    def block_of(j, k, side):
        return blocks_of(j) + 2 * quarter(k) + side

    def ax_copy(j, n, side):
        block = block_of(j, 0, side)
        at = n if n == side else 2
        return remote(act.at[block], act.at[block], sent.at[3], ax_r.at[j, at], xpeer(toward[n]))

    def ax_relay(j, n):
        block = block_of(j, toward[1 - n], n)
        return remote(act.at[block], act.at[block], sent.at[3], ax_r.at[j, 2], xpeer(toward[n]))

    def activate(j):
        pz_copy(j).wait_recv()
        for side in (0, 1):
            pre = z_own[j, side] + z_in[j, side].astype(F32) + bias_ref[...]
            act[block_of(j, 0, side)] = jnp.maximum(pre, 0.0).astype(BF16)
        for side in (0, 1):
            for n in (0, 1):
                ax_copy(j, n, n if side == 0 else 1 - n).start()

    def relay(j):
        ax_copy(j, 0, 0).wait_recv()
        ax_relay(j, 0).start()
        ax_copy(j, 1, 1).wait_recv()
        ax_relay(j, 1).start()

    def guz_copy(h):
        return remote(gu_zsend.at[h], gu_zin.at[h], sent.at[1], guz_r.at[h], zpeer)

    def gu_reduce(h):
        remote(gu_in.at[h], gu_in.at[h], sent.at[1], gux_r.at[h, 2], mate).wait_recv()
        for keep in (0, 1):
            half = 1 - zh if keep == 0 else zh
            mine = gu_rows(h, 0, half)
            total = gu_own[mine, :] + gu_in[h, half, 0] + gu_in[h, half, 1]
            if keep == 0:
                gu_zsend[h] = total.astype(BF16)
                guz_copy(h).start()
            else:
                gu_own[mine, :] = total

    def hid_of(h, k, side):
        return h * 8 + 2 * quarter(k) + side

    def hz_copy(h):
        part = hid_of(h, 0, zh)
        return remote(hid.at[part], hid.at[part], sent.at[4], hz_r.at[h], zpeer)

    def hx_copy(h, n, second):
        part = hid_of(h, 0, (1 - zh) if second else zh)
        at = n if n == second else 2
        return remote(hid.at[part], hid.at[part], sent.at[4], hx_r.at[h, at], xpeer(toward[n]))

    def hx_relay(h, n):
        part = hid_of(h, toward[1 - n], zh if n == 0 else 1 - zh)
        return remote(hid.at[part], hid.at[part], sent.at[4], hx_r.at[h, 2], xpeer(toward[n]))

    def gu_activate(h):
        guz_copy(h).wait_recv()
        total = gu_own[gu_rows(h, 0, zh), :] + gu_zin[h].astype(F32)
        gate, up = total[:, :HIDDEN], total[:, HIDDEN:]
        hid[hid_of(h, 0, zh)] = (gate / (1.0 + jnp.exp(-gate)) * up).astype(BF16)
        hz_copy(h).start()
        for n in (0, 1):
            hx_copy(h, n, 0).start()

    def gu_pass_on(h):
        hz_copy(h).wait_recv()
        for n in (1, 0):
            hx_copy(h, n, 1).start()

    def hid_relay(h):
        hx_copy(h, 0, 0).wait_recv()
        hx_relay(h, 0).start()
        hx_copy(h, 1, 1).wait_recv()
        hx_relay(h, 1).start()

    def out_copy(k):
        there = (e + k) % EXPERTS
        return remote(
            out_send.at[k], out_in.at[e], sent.at[5], out_r.at[0], {"exp": there, "feat": f}
        )

    def down(h):
        four = hid.at[pl.ds(0, 4)]
        remote(four, four, sent.at[4], hx_r.at[h, 2], mate).wait_recv()
        hidden = hid[pl.ds(h * 8, 8)].reshape(128, HIDDEN)
        for n in range(7):
            cols = pl.ds(n * 128, 128)
            out_send[pl.ds(h * 16, 16), :, cols] = (
                dot(hidden, down_w[:, cols]).reshape(16, SLOT, 128).astype(BF16)
            )
        if h == 0:
            out_in[e] = out_send[0]

        def start(k, carry):
            out_copy(k).start()
            return carry

        lax.fori_loop(1 if h == 0 else 16, h * 16 + 16, start, 0)

    def cm_copy(j):
        return remote(rec.at[j, 1 - core], mate_in.at[j], sent.at[6], cm_r.at[j], mate)

    def decode(j):
        four = act.at[pl.ds(0, 4)]
        remote(four, four, sent.at[3], ax_r.at[j, 2], mate).wait_recv()
        rows = act[pl.ds(blocks_of(j), 8)].reshape(CHUNK_ROWS, FEATURES)

        def tile(n, carry):
            at = pl.multiple_of(n * 256, 256)
            part = dot(rows, dec_w[:, pl.ds(at, 256)]).reshape(4, 2, ROWS, 256)
            for c in (0, 1):
                rec[j, c, :, :, pl.ds(at, 256)] = part[:, c]
            return carry

        lax.fori_loop(0, WIDE // 256, tile, 0)
        cm_copy(j).start()

    def fin_copy(j):
        return remote(
            fin_send.at[j], fin_in.at[j], sent.at[7], fin_r.at[0], same_core((y + j) % 4, zl)
        )

    def fin_z_copy(k):
        return remote(
            fin_zsend.at[k], fin_zin.at[k], sent.at[7], fin_r.at[1], same_core(y, (zl + k) % 4)
        )

    def finish(j):
        cm_copy(j).wait_recv()
        for to in range(4):
            total = rec[j, core, to] + mate_in[j, to]
            if j == 0:
                fin_own[to] = total
            else:
                fin_send[j, to] = total.astype(BF16)
        if j > 0:
            fin_copy(j).start()

    def finish_z():
        most = fin_in.at[pl.ds(1, 3)]
        remote(most, most, sent.at[7], fin_r.at[0], mate).wait_recv()
        for k in (1, 3, 2, 0):
            to = (zl + k) % 4
            total = fin_own[to]
            for j in range(1, CHUNKS):
                total = total + fin_in[j, to].astype(F32)
            if k == 0:
                fin_zin[0] = total
            else:
                fin_zsend[k] = total
                fin_z_copy(k).start()

    def row_mate_copy():
        return remote(row_own, row_mate, sent.at[8], rm_r.at[0], mate)

    def row_y_copy(k):
        there = (y + k) % 4
        return remote(
            row_part.at[there], row_in.at[k - 1], sent.at[8], ry_r.at[k - 1], same_core(there, zl)
        )

    def row_z_copy(k):
        return remote(
            row_sum, row_zin.at[k - 1], sent.at[8], rz_r.at[k - 1], same_core(y, (zl + k) % 4)
        )

    def row_gather_copy(k):
        return remote(
            rows_dec.at[y], rows_dec.at[y], sent.at[8], rg_r.at[k - 1], same_core((y + k) % 4, zl)
        )

    def rows_start():
        mine = lax.dot_general(
            dec_w[:, pl.ds(WIDTH, EXTRA)],
            dec_w[:, pl.ds(0, WIDTH)],
            (((0,), (0,)), ((), ())),
            preferred_element_type=F32,
        )
        row_own[...] = mine[:64].astype(BF16).reshape(4, ROWS, WIDTH)
        row_mate_copy().start()

    def rows_y():
        row_mate_copy().wait_recv()
        row_part[...] = (row_own[...].astype(F32) + row_mate[...].astype(F32)).astype(BF16)
        for k in range(1, 4):
            row_y_copy(k).start()

    def rows_z():
        total = row_part[y].astype(F32)
        for k in range(1, 4):
            row_y_copy(k).wait_recv()
            total = total + row_in[k - 1].astype(F32)
        row_sum[...] = total.astype(BF16)
        for k in range(1, 4):
            row_z_copy(k).start()

    def rows_gather():
        total = row_sum[...].astype(F32)
        for k in range(1, 4):
            row_z_copy(k).wait_recv()
            total = total + row_zin[k - 1].astype(F32)
        rows_dec[y] = total.astype(BF16)
        for k in range(1, 4):
            row_gather_copy(k).start()

    def combine_moe():
        most = out_in.at[pl.ds(1, EXPERTS - 1)]
        remote(most, most, sent.at[5], out_r.at[0], mate).wait_recv()
        for n in range(7):
            cols = pl.ds(n * 128, 128)
            rows = out_in[:, :, cols].astype(F32).reshape(EXPERTS * SLOT, 128).astype(BF16)
            moe_ref[:, cols] = dot(combine[2], rows) + dot(combine[1], rows) + dot(combine[0], rows)
        write_moe.start()

    def total_up():
        most = fin_zin.at[pl.ds(1, 3)]
        remote(most, most, sent.at[7], fin_r.at[1], mate).wait_recv()
        total = (fin_zin[0] + fin_zin[1]) + (fin_zin[2] + fin_zin[3])
        recon_ref[...] = total[:, :WIDTH]
        write_recon.start()
        for k in range(1, 4):
            row_gather_copy(k).wait_recv()
        small[4].wait()
        change = values_ref[...].astype(F32) - total[:, WIDTH : WIDTH + clamps]
        listed = rows_dec[...].reshape(64, WIDTH)
        high, middle, low = three(change)
        shift_ref[...] = dot(low, listed) + dot(middle, listed) + dot(high, listed)
        write_shift.start()

    write_recon = pltpu.make_async_copy(recon_ref, recon_hbm, load_sem.at[11])
    write_moe = pltpu.make_async_copy(moe_ref, moe_hbm, load_sem.at[12])
    write_shift = pltpu.make_async_copy(shift_ref, shift_hbm, load_sem.at[13])

    from_mate(0)
    load_enc.wait()
    pre_multiply(0)
    for k in (1, 3, 2):
        from_y(k)
    for k in (1, 3, 2):
        from_mate(k)
    gu_pick()
    pre_relay(0)
    pre_multiply(1)
    gu_multiply(1)
    pre_multiply(2)
    pre_reduce(0)
    pre_relay(1)
    gu_multiply(0)
    load_dec.wait()
    listed_columns()
    rows_start()
    gu_relay(1)
    pre_multiply(3)
    rows_y()
    route_weights()
    pre_relay(2)
    rows_z()
    small[5].wait()
    activate(0)
    pre_reduce(1)
    gu_relay(0)
    rows_gather()
    gu_reduce(1)
    pre_relay(3)
    activate(1)
    pre_reduce(2)
    relay(0)
    gu_activate(1)
    gu_reduce(0)
    pre_reduce(3)
    relay(1)
    activate(2)
    decode(0)
    gu_pass_on(1)
    decode(1)
    gu_activate(0)
    relay(2)
    finish(0)
    hid_relay(1)
    finish(1)
    activate(3)
    decode(2)
    gu_pass_on(0)
    load_down.wait()
    down(1)
    relay(3)
    finish(2)
    hid_relay(0)
    decode(3)
    down(0)
    finish(3)
    finish_z()
    combine_moe()
    total_up()

    for kind, ref in (
        (0, tok_all.at[pl.ds(0, 31)]),
        (1, gu_own.at[pl.ds(0, 208)]),
        (2, act),
        (3, act.at[pl.ds(0, 24)]),
        (4, hid.at[pl.ds(0, 14)]),
        (5, out_send.at[pl.ds(1, 31)]),
        (6, mate_in),
        (7, tok_all.at[pl.ds(0, 18)]),
        (8, out_send.at[pl.ds(0, 26)]),
    ):
        remote(ref, ref, sent.at[kind], rm_r.at[0], mate).wait_send()
    for write in (write_recon, write_moe, write_shift):
        write.wait()


def fused(*operands):
    hbm = pl.BlockSpec(memory_space=pl.ANY)
    dma = pltpu.SemaphoreType.DMA
    scratch = [
        pltpu.VMEM((8, ROWS), jnp.int32),
        pltpu.VMEM((8, ROWS), F32),
        pltpu.VMEM((1, FEATURES), F32),
        pltpu.VMEM(operands[4].shape, jnp.int32),
        pltpu.VMEM(operands[5].shape, BF16),
        pltpu.VMEM((ROWS, WIDTH), F32),
        pltpu.VMEM((ROWS, WIDTH), F32),
        pltpu.VMEM((ROWS, WIDTH), F32),
        pltpu.VMEM((EXPERTS * SLOT, WIDTH), BF16),
        pltpu.VMEM((WIDTH, HIDDEN), BF16),
        pltpu.VMEM((WIDTH, HIDDEN), BF16),
        pltpu.VMEM((HIDDEN, WIDTH), BF16),
        pltpu.VMEM((WIDTH, FEATURES), BF16),
        pltpu.VMEM((FEATURES, WIDE), BF16),
        pltpu.VMEM((EXPERTS, ROWS, WIDE), BF16),
        pltpu.VMEM((EXPERTS * SLOT, 2 * HIDDEN), F32),
        pltpu.VMEM((2, 2, ROWS, 2 * HIDDEN), F32),
        pltpu.VMEM((2, 2, 2, ROWS, 2 * HIDDEN), F32),
        pltpu.VMEM((2, ROWS, 2 * HIDDEN), BF16),
        pltpu.VMEM((2, ROWS, 2 * HIDDEN), BF16),
        pltpu.VMEM((CHUNKS, CHUNK_ROWS, FEATURES), F32),
        pltpu.VMEM((CHUNKS, CHUNK_ROWS, FEATURES), BF16),
        pltpu.VMEM((CHUNKS, 2, ROWS, FEATURES), BF16),
        pltpu.VMEM((CHUNKS, 2, 2, ROWS, FEATURES), BF16),
        pltpu.VMEM((CHUNKS, 2, ROWS, FEATURES), BF16),
        pltpu.VMEM((CHUNKS, 2, ROWS, FEATURES), BF16),
        pltpu.VMEM((CHUNKS, 2, ROWS, FEATURES), F32),
        pltpu.VMEM((EXPERTS, ROWS, FEATURES), BF16),
        pltpu.VMEM((2 * 8, ROWS, HIDDEN), BF16),
        pltpu.VMEM((EXPERTS, SLOT, WIDTH), BF16),
        pltpu.VMEM((EXPERTS, SLOT, WIDTH), BF16),
        pltpu.VMEM((CHUNKS, 2, 4, ROWS, WIDE), F32),
        pltpu.VMEM((CHUNKS, 4, ROWS, WIDE), F32),
        pltpu.VMEM((CHUNKS, 4, ROWS, WIDE), BF16),
        pltpu.VMEM((CHUNKS, 4, ROWS, WIDE), BF16),
        pltpu.VMEM((4, ROWS, WIDE), F32),
        pltpu.VMEM((4, ROWS, WIDE), F32),
        pltpu.VMEM((4, ROWS, WIDE), F32),
        pltpu.VMEM((3, ROWS, EXPERTS * SLOT), BF16),
        pltpu.VMEM((4, ROWS, WIDTH), BF16),
        pltpu.VMEM((4, ROWS, WIDTH), BF16),
        pltpu.VMEM((4, ROWS, WIDTH), BF16),
        pltpu.VMEM((3, ROWS, WIDTH), BF16),
        pltpu.VMEM((ROWS, WIDTH), BF16),
        pltpu.VMEM((3, ROWS, WIDTH), BF16),
        pltpu.VMEM((4, ROWS, WIDTH), BF16),
        dma((14,)),
        dma((9,)),
        dma((3,)),
        dma((12,)),
        dma((4,)),
        dma((2, 3)),
        dma((2,)),
        dma((2,)),
        dma((2, 3)),
        dma((CHUNKS, 3)),
        dma((CHUNKS,)),
        dma((CHUNKS, 3)),
        dma((1,)),
        dma((CHUNKS,)),
        dma((2,)),
        dma((1,)),
        dma((3,)),
        dma((3,)),
        dma((3,)),
    ]
    return pl.pallas_call(
        kernel,
        out_shape=(
            jax.ShapeDtypeStruct((ROWS, WIDTH), F32),
            jax.ShapeDtypeStruct((ROWS, WIDTH), F32),
            jax.ShapeDtypeStruct((ROWS, WIDTH), F32),
        ),
        in_specs=[hbm] * 11,
        out_specs=(hbm, hbm, hbm),
        scratch_shapes=scratch,
        name="fused_layer",
        cost_estimate=pl.CostEstimate(
            flops=6_000_000_000, bytes_accessed=400_000_000, transcendentals=0
        ),
        compiler_params=pltpu.CompilerParams(
            collective_id=0, has_side_effects=True, vmem_limit_bytes=56 << 20
        ),
    )(*operands)


def local(
    tokens,
    route_ids,
    route_weights,
    gate_proj,
    up_proj,
    down_proj,
    enc_weight,
    enc_bias,
    dec_weight,
    dec_bias,
    clamp_ids,
    clamp_values,
):
    recon, moe_out, shift = fused(
        tokens,
        route_ids.T,
        route_weights.T,
        enc_bias[None, :],
        clamp_ids[None, :],
        clamp_values[None, :],
        gate_proj,
        up_proj,
        down_proj,
        enc_weight,
        dec_weight,
    )
    return moe_out - recon - dec_bias, moe_out + shift


def solution(mesh):
    placed = (
        P("exp", "feat"),
        P("exp", None),
        P("exp", None),
        P("exp", "feat", None),
        P("exp", "feat", None),
        P("exp", None, "feat"),
        P("feat", "exp"),
        P("exp"),
        P("exp", "feat"),
        P("feat"),
        P(),
        P(),
    )
    return jax.shard_map(
        local,
        mesh=mesh,
        in_specs=placed,
        out_specs=(P("exp", "feat"), P("exp", "feat")),
        check_vma=False,
    )
```
